32 devices in a mesh: ctx: 8 (over y, x, core), tp: 4 (over z).
Axes of the slice: x: 2, y: 2, z: 4, core: 2. Of those that a mesh axis runs over, the one named last changes fastest.
Arguments:
- query_proj: bfloat16 [8192, 8192], P('ctx', 'tp'), may hold values from -6 to 6
- key_proj: bfloat16 [8192, 8192], P('ctx', 'tp'), may hold values from -6 to 6
- value_proj: bfloat16 [8192, 8192], P('ctx', 'tp'), may hold values from -6 to 6
- cotangent: bfloat16 [8192, 8192], P('ctx', 'tp'), may hold values from -6 to 6
- short_taps: float32 [3, 3, 8192], P(None, None, 'tp'), may hold values from -2.5 to 2.5
- residues: float32 [512, 16], P('tp'), may hold values from -0.6 to 0.6
- decay_rates: float32 [512, 16], P('tp'), may hold values from 3.6621095e-05 to 0.08
Outputs:
- mixed: bfloat16 [8192, 8192], P('ctx', 'tp')
- grad_query: bfloat16 [8192, 8192], P('ctx', 'tp')
- grad_key: bfloat16 [8192, 8192], P('ctx', 'tp')
- grad_value: bfloat16 [8192, 8192], P('ctx', 'tp')
- grad_taps: float32 [3, 3, 8192], P(None, None, 'tp')
- grad_residues: float32 [512, 16], P('tp')
The draws below stay inside these ranges and needn't reach their ends.
All inputs are finite; a program needn't handle non-finite values.
Results may differ from the reference program's by a relative error of at most 0.014.
Values may be sent and summed in bfloat16 or wider, within the bound.
No kernel may reach another device: no remote copies, remote signals or barrier semaphores. Data moves between devices by JAX's collectives and lax.ppermute only.
A program may use at most 128 MiB of HBM per device.

```python
import math
import jax
import jax.numpy as jnp
from jax import lax

D = 8192
TAPS = 3
MODES = 16
FILTER_GROUPS = 512
SEQ = 8192


def level_of(stream_key, shape, split, smallest, largest):
    loudness, own = 1.0, jax.random.fold_in(stream_key, 6)
    for position, parts in split:
        steps = jnp.exp(jax.random.uniform(jax.random.fold_in(own, position), (parts,), jnp.float32, smallest / len(split), largest / len(split)))
        loudness = loudness * jnp.repeat(steps, shape[position] // parts).reshape([-1 if axis == position else 1 for axis in range(len(shape))])
    return loudness


def scatter_about(stream_key, extent, scale, limit, pieces=(), kind=jnp.bfloat16):
    array = scale * jax.random.normal(stream_key, extent, jnp.float32)
    if pieces:
        array = array * level_of(stream_key, extent, pieces, -0.22, 0.18)
    return jnp.clip(array, -limit, limit).astype(kind)


def setup_inputs(seed: int = 0) -> dict:
    key_list = jax.random.split(jax.random.key(seed), 8)
    return {
        "query_proj": scatter_about(key_list[0], (SEQ, D), 1.0, 6.0, ((0, 8), (1, 4))),
        "key_proj": scatter_about(key_list[1], (SEQ, D), 1.0, 6.0, ((0, 8), (1, 4))),
        "value_proj": scatter_about(key_list[2], (SEQ, D), 1.0, 6.0, ((0, 8), (1, 4))),
        "cotangent": scatter_about(key_list[3], (SEQ, D), 1.0, 6.0, ((0, 8), (1, 4))),
        "short_taps": scatter_about(key_list[4], (3, TAPS, D), 0.6, 2.5, ((2, 4),), jnp.float32),
        "residues": scatter_about(key_list[5], (FILTER_GROUPS, MODES), 0.1, 0.6, ((0, 4),), jnp.float32),
        "decay_rates": jnp.clip(jnp.exp(math.log(0.08) - 7.6891574 * jax.random.uniform(key_list[6], (FILTER_GROUPS, MODES), jnp.float32) ** level_of(key_list[6], (FILTER_GROUPS, MODES), ((0, 4),), -0.2, 0.2)), 3.662109520519152e-05, 0.08),
    }


def kernel_tables(residues, decay_rates, block_len):
    offsets = jnp.arange(block_len, dtype=jnp.float32)
    spread = offsets[:, None] - offsets[None, :]
    causal = spread >= 0.0
    lagged = jnp.maximum(spread, 0.0)
    toeplitz = jnp.zeros((residues.shape[0], block_len, block_len), jnp.float32)
    for mode_index in range(residues.shape[1]):
        rate = decay_rates[:, mode_index][:, None, None]
        toeplitz = toeplitz + residues[:, mode_index][:, None, None] * jnp.exp(-rate * lagged[None])
    toeplitz = jnp.where(causal[None], toeplitz, jnp.zeros_like(toeplitz))
    readin = residues[:, :, None] * jnp.exp(-decay_rates[:, :, None] * (offsets + 1.0)[None, None, :])
    absorb = jnp.exp(-decay_rates[:, :, None] * (block_len - 1.0 - offsets)[None, None, :])
    passing = jnp.exp(-decay_rates * block_len)
    return (toeplitz, readin, absorb, passing)

def state_combine(earlier, later):
    return (earlier[0] * later[0], later[1] + later[0] * earlier[1])

def modal_conv(columns, residues, decay_rates):
    width, length = columns.shape
    groups, modes = residues.shape
    members = width // groups
    block_len = min(128, length)
    count = length // block_len
    toeplitz, readin, absorb, passing = kernel_tables(residues, decay_rates, block_len)
    blocks = columns.reshape(groups, members, count, block_len)
    inner = jnp.einsum('gts,gkns->gknt', toeplitz, blocks, precision=lax.Precision.HIGHEST)
    ends = jnp.einsum('gms,gkns->nmgk', absorb, blocks, precision=lax.Precision.HIGHEST).reshape(count, modes, width)
    rate_columns = jnp.repeat(passing.T, members, axis=1)
    factors = jnp.broadcast_to(rate_columns[None], (count, modes, width))
    after_block = lax.associative_scan(state_combine, (factors, ends), axis=0)[1]
    before = jnp.concatenate([jnp.zeros((1, modes, width), jnp.float32), after_block[:-1]], axis=0)
    carried = jnp.einsum('gmt,nmgk->gknt', readin, before.reshape(count, modes, groups, members), precision=lax.Precision.HIGHEST)
    return ((inner + carried).reshape(width, length), after_block[-1])

def short_forward(stream, prior, taps):
    span = taps.shape[0] - 1
    length = stream.shape[0]
    extended = jnp.concatenate([prior, stream], axis=0)
    total = jnp.zeros(stream.shape, jnp.float32)
    for lag_index in range(taps.shape[0]):
        window = extended[span - lag_index:span - lag_index + length].astype(jnp.float32)
        total = total + taps[lag_index][None, :] * window
    return total

def short_backward(grad_out, after, stream, prior, taps):
    span = taps.shape[0] - 1
    length = stream.shape[0]
    extended = jnp.concatenate([prior, stream], axis=0)
    extended_grad = jnp.concatenate([grad_out, after], axis=0)
    grad_in = jnp.zeros(grad_out.shape, jnp.float32)
    tap_rows = []
    for lag_index in range(taps.shape[0]):
        grad_in = grad_in + taps[lag_index][None, :] * extended_grad[lag_index:lag_index + length]
        window = extended[span - lag_index:span - lag_index + length].astype(jnp.float32)
        tap_rows.append(lax.optimization_barrier(jnp.sum(grad_out * window, axis=0)))
    return (grad_in, jnp.stack(tap_rows))

def reference(query_proj, key_proj, value_proj, cotangent, short_taps, residues, decay_rates):
    span = TAPS - 1
    prior = jnp.zeros((span, D), jnp.bfloat16)
    after = jnp.zeros((span, D), jnp.float32)
    query_short = short_forward(query_proj, prior, short_taps[0])
    key_short = short_forward(key_proj, prior, short_taps[1])
    value_short = short_forward(value_proj, prior, short_taps[2])
    gated_low = (key_short * value_short).astype(jnp.bfloat16)
    gated_cols = lax.optimization_barrier(gated_low.T).astype(jnp.float32)
    outputs, unwind = jax.vjp(lambda signal, weights: modal_conv(signal, weights, decay_rates), gated_cols, residues)
    long_cols, final = outputs
    long_low = long_cols.T.astype(jnp.bfloat16)
    long_out = lax.optimization_barrier(long_low).astype(jnp.float32)
    mixed = (query_short * long_out).astype(jnp.bfloat16)
    grad_cot = cotangent.astype(jnp.float32)
    grad_qshort = grad_cot * long_out
    grad_long_low = (grad_cot * query_short).astype(jnp.bfloat16)
    grad_long_cols = lax.optimization_barrier(grad_long_low.T).astype(jnp.float32)
    grad_gated_cols, grad_residues = unwind((grad_long_cols, jnp.zeros_like(final)))
    grad_gated_low = grad_gated_cols.T.astype(jnp.bfloat16)
    grad_gated = lax.optimization_barrier(grad_gated_low).astype(jnp.float32)
    grad_kshort = grad_gated * value_short
    grad_vshort = grad_gated * key_short
    grad_query, taps_query = short_backward(grad_qshort, after, query_proj, prior, short_taps[0])
    grad_key, taps_key = short_backward(grad_kshort, after, key_proj, prior, short_taps[1])
    grad_value, taps_value = short_backward(grad_vshort, after, value_proj, prior, short_taps[2])
    grad_taps = jnp.stack([taps_query, taps_key, taps_value])
    return (mixed, grad_query.astype(jnp.bfloat16), grad_key.astype(jnp.bfloat16), grad_value.astype(jnp.bfloat16), grad_taps, grad_residues)
```

```python
import functools
import jax
import jax.numpy as jnp
from jax import lax
from jax.experimental import pallas as pl
from jax.experimental.pallas import tpu as pltpu
from jax.sharding import PartitionSpec as P

F32 = jnp.float32
BF16 = jnp.bfloat16
BLOCK = 128
LANES = 128
PAD = 8
HIGHEST = lax.Precision.HIGHEST


def dot(a, b, a_dim=1, b_dim=0, precision=None):
    return lax.dot_general(
        a, b, (((a_dim,), (b_dim,)), ((), ())), precision=precision, preferred_element_type=F32
    )


def iota(shape, axis):
    return lax.broadcasted_iota(jnp.int32, shape, axis)


def split(value):
    high = value.astype(BF16)
    return high, (value - high.astype(F32)).astype(BF16)


def eye():
    shape = (BLOCK, BLOCK)
    return (iota(shape, 0) == iota(shape, 1)).astype(F32).astype(BF16)


def fill_streams(streams, prior_ref, us, length):
    span = prior_ref.shape[0] // len(streams)
    for i, ref in enumerate(streams):
        us[i, PAD - span : PAD, :] = prior_ref[i * span : (i + 1) * span, :].astype(F32)
        us[i, PAD : PAD + length, :] = ref[...].astype(F32)


def windows(us, i, start, rows, taps):
    return [us[i, PAD + start - j : PAD + start - j + rows, :] for j in range(taps)]


def short(taps_ref, i, wins):
    taps = len(wins)
    total = taps_ref[i * taps : i * taps + 1, :] * wins[0]
    for j in range(1, taps):
        total = total + taps_ref[i * taps + j : i * taps + j + 1, :] * wins[j]
    return total


def states_kernel(
    sizes, me_ref, q_ref, k_ref, v_ref, c_ref, prior_ref, taps_ref, rate_col, rate_row,
    x_ref, h_ref, ef_ref, eb_ref, send_ref, us, gs, ls, af, ab,
):
    members, modes, taps, ctx = sizes
    length = q_ref.shape[0]
    count, groups = length // BLOCK, LANES // members
    width = groups * modes

    @pl.when(pl.program_id(0) == 0)
    def _():
        af[...] = jnp.zeros_like(af)
        ab[...] = jnp.zeros_like(ab)

    step = iota((width, BLOCK), 1).astype(F32)
    rate = rate_col[...]
    for table, array in ((af, jnp.exp(-rate * (BLOCK - 1.0 - step))), (ab, jnp.exp(-rate * step))):
        high, low = split(array)
        for g in range(groups):
            rows = slice(g * modes, (g + 1) * modes)
            lanes = slice(g * BLOCK, (g + 1) * BLOCK)
            table[g * modes : (g + 1) * modes, lanes] = high[rows]
            table[width + g * modes : width + (g + 1) * modes, lanes] = low[rows]
    fill_streams((q_ref, k_ref, v_ref), prior_ref, us, length)
    unit = eye()
    half = BLOCK // 2
    for n in range(count):
        for part in range(2):
            start = n * BLOCK + part * half
            rows = slice(start, start + half)
            query = short(taps_ref, 0, windows(us, 0, start, half, taps))
            key = short(taps_ref, 1, windows(us, 1, start, half, taps))
            value = short(taps_ref, 2, windows(us, 2, start, half, taps))
            gs[rows, :] = (key * value).astype(BF16)
            ls[rows, :] = (c_ref[rows, :].astype(F32) * query).astype(BF16)
        for source, target in ((gs, x_ref), (ls, h_ref)):
            turned = dot(unit, source[n * BLOCK : (n + 1) * BLOCK, :], 1, 1).astype(BF16)
            for g in range(groups):
                target[n * members : (n + 1) * members, g * BLOCK : (g + 1) * BLOCK] = turned[
                    g * members : (g + 1) * members
                ]
    decay = jnp.exp(-rate_row[0] * float(BLOCK))
    forward = dot(x_ref[...], af[...], 1, 1)
    forward = forward[:, :width] + forward[:, width:]
    backward = dot(h_ref[...], ab[...], 1, 1)
    backward = backward[:, :width] + backward[:, width:]
    ef_ref[...] = forward
    eb_ref[...] = backward
    last = jnp.zeros((members, width), F32)
    first = jnp.zeros((members, width), F32)
    for n in range(count):
        m = count - 1 - n
        last = decay * last + forward[n * members : (n + 1) * members]
        first = decay * first + backward[m * members : (m + 1) * members]
    me = me_ref[0]
    for j in range(ctx):
        send_ref[j] = jnp.where(j > me, last, first)


def inner_kernel(sizes, x_ref, h_ref, rate_col, res_col, y_ref, z_ref, grad_ref):
    members, modes, taps, ctx = sizes
    groups = LANES // members
    width = groups * modes
    step = iota((width, BLOCK), 1).astype(F32)
    rate, res = rate_col[...], res_col[...]
    rising = jnp.exp(-rate * (BLOCK - 1.0 - step))
    falling = res * jnp.exp(-rate * step)
    reverse = res * rising
    row, col = iota((BLOCK, BLOCK), 0), iota((BLOCK, BLOCK), 1)
    upper, lower, causal = col >= row, col <= row, row + col < BLOCK
    flip = (row + col == BLOCK - 1).astype(F32).astype(BF16)
    sums = []
    for g in range(groups):
        lanes = slice(g * BLOCK, (g + 1) * BLOCK)
        rows = slice(g * modes, (g + 1) * modes)
        taps_up = jnp.broadcast_to(jnp.sum(falling[rows], axis=0, keepdims=True), (BLOCK, BLOCK))
        taps_down = jnp.broadcast_to(jnp.sum(reverse[rows], axis=0, keepdims=True), (BLOCK, BLOCK))
        up = jnp.where(upper, pltpu.roll(taps_up, 0, 1, stride=1, stride_axis=0), 0.0).astype(BF16)
        down = jnp.where(lower, pltpu.roll(taps_down, 1, 1, stride=1, stride_axis=0), 0.0).astype(BF16)
        x, h = x_ref[:, lanes], h_ref[:, lanes]
        y_ref[:, lanes] = dot(x, up).astype(BF16)
        z_ref[:, lanes] = dot(h, down).astype(BF16)
        turned = dot(flip, h, 1, 1).astype(BF16)
        pairs = jnp.where(causal, dot(turned, x), 0.0)
        pairs = pltpu.roll(pairs, 0, 1, stride=1, stride_axis=0)
        sums.append(jnp.sum(pairs, axis=0, keepdims=True))
    crossed = dot(jnp.concatenate(sums, axis=0), rising, 1, 1, HIGHEST)
    own = iota((groups, width), 1) // modes == iota((groups, width), 0)
    grad_ref[0] = jnp.sum(jnp.where(own, crossed, 0.0), axis=0, keepdims=True)


def finish_kernel(
    sizes, me_ref, q_ref, k_ref, v_ref, c_ref, prior_ref, after_ref, taps_ref, rate_row, res_row,
    lag_ref, y_ref, z_ref, ef_ref, eb_ref, recv_ref, near_ref,
    mixed_ref, gq_ref, gk_ref, gv_ref, terms_ref, us, es, lo, gg,
):
    members, modes, taps, ctx = sizes
    length = q_ref.shape[0]
    count, groups = length // BLOCK, LANES // members
    width = groups * modes
    span = taps - 1
    rate, res = rate_row[0], res_row[0]
    me = me_ref[0]
    whole, decay = jnp.exp(-rate * float(length)), jnp.exp(-rate * float(BLOCK))
    ahead = jnp.zeros((members, width), F32)
    behind = jnp.zeros((members, width), F32)
    for i in range(ctx - 1):
        j = ctx - 1 - i
        ahead = jnp.where(i < me, whole * ahead + recv_ref[i], ahead)
        behind = jnp.where(j > me, whole * behind + recv_ref[j], behind)
    incoming = behind
    forward, backward = [], [None] * count
    for n in range(count):
        m = count - 1 - n
        forward.append(ahead)
        ahead = decay * ahead + ef_ref[n * members : (n + 1) * members, :]
        backward[m] = behind
        behind = decay * behind + eb_ref[m * members : (m + 1) * members, :]
    cross = forward[0] * eb_ref[0:members, :]
    for n in range(1, count):
        cross = cross + forward[n] * eb_ref[n * members : (n + 1) * members, :]
    grad_res = jnp.exp(-rate) * jnp.sum(cross, axis=0, keepdims=True) + lag_ref[0]

    step = iota((BLOCK, width), 0).astype(F32)
    unit = eye()
    lane_group = iota((members, width), 1) // modes
    for table, states, source, target in (
        (res * jnp.exp(-rate * (step + 1.0)), forward, y_ref, lo),
        (res * jnp.exp(-rate * (BLOCK - step)), backward, z_ref, gg),
    ):
        high, low = split(table)
        left = jnp.concatenate([unit, high, high, low], axis=1)
        for n in range(count):
            s_high = states[n].astype(BF16).astype(F32)
            s_low = states[n] - s_high
            rows = []
            for g in range(groups):
                own = lane_group == g
                wide = jnp.where(own, s_high, 0.0).astype(BF16)
                fine = jnp.where(own, s_low, 0.0).astype(BF16)
                piece = source[n * members : (n + 1) * members, g * BLOCK : (g + 1) * BLOCK]
                rows.append(jnp.concatenate([piece, wide, fine, wide], axis=1))
            right = jnp.concatenate(rows, axis=0)
            target[n * BLOCK : (n + 1) * BLOCK, :] = dot(left, right, 1, 1).astype(BF16)

    fill_streams((q_ref, k_ref, v_ref), prior_ref, us, length)
    rest = jnp.zeros((PAD - span, LANES), F32)
    head = after_ref[...].astype(F32)
    for i in range(3):
        us[i, PAD + length : 2 * PAD + length, :] = jnp.concatenate(
            [head[i * span : (i + 1) * span], rest], axis=0
        )
    cot = jnp.concatenate([head[3 * span : 4 * span], rest], axis=0)
    query = short(taps_ref, 0, windows(us, 0, length, PAD, taps))
    key = short(taps_ref, 1, windows(us, 1, length, PAD, taps))
    value = short(taps_ref, 2, windows(us, 2, length, PAD, taps))
    line = jnp.zeros((1, LANES), F32)
    second = iota((PAD, LANES), 0) == 1
    gated = (key * value).astype(BF16).astype(F32)
    grad_long = (cot * query).astype(BF16).astype(F32)
    gated_prev = jnp.where(second, jnp.concatenate([line, gated[:-1]], axis=0), 0.0)
    grad_prev = jnp.where(second, jnp.concatenate([line, grad_long[:-1]], axis=0), 0.0)
    order = iota((PAD, width), 0).astype(F32)

    def spread(state):
        return jnp.concatenate(
            [jnp.where(lane_group == g, state, 0.0) for g in range(groups)], axis=0
        )

    out = dot(res * jnp.exp(-rate * (order + 1.0)), spread(ahead), 1, 1, HIGHEST)
    out = out + near_ref[0:1, :] * gated + near_ref[1:2, :] * gated_prev
    out = out.astype(BF16).astype(F32)
    back = dot(res * jnp.exp(rate * order), spread(incoming), 1, 1, HIGHEST)
    back = back - near_ref[2:3, :] * grad_prev
    back = back.astype(BF16).astype(F32)
    for i, edge in enumerate((cot * out, back * value, back * key)):
        es[i, length : length + PAD, :] = edge

    part = BLOCK // 2
    sums = [jnp.zeros((8, LANES), F32) for _ in range(3 * taps)]
    for n in reversed(range(length // part)):
        start = n * part
        rows = slice(start, start + part)
        long_out, grad_gated = lo[rows, :].astype(F32), gg[rows, :].astype(F32)
        wins = [windows(us, i, start, part, taps) for i in range(3)]
        query, key, value = [short(taps_ref, i, wins[i]) for i in range(3)]
        mixed_ref[rows, :] = (query * long_out).astype(BF16)
        edges = (c_ref[rows, :].astype(F32) * long_out, grad_gated * value, grad_gated * key)
        for i, (edge, target) in enumerate(zip(edges, (gq_ref, gk_ref, gv_ref))):
            es[i, rows, :] = edge
            total = taps_ref[i * taps : i * taps + 1, :] * edge
            for j in range(1, taps):
                total = total + taps_ref[i * taps + j : i * taps + j + 1, :] * es[
                    i, start + j : start + j + part, :
                ]
            target[rows, :] = total.astype(BF16)
            for j in range(taps):
                product = edge * wins[i][j]
                sums[i * taps + j] = sums[i * taps + j] + jnp.sum(
                    product.reshape(part // 8, 8, LANES), axis=0
                )
    high, low = split(grad_res)
    lines = [jnp.sum(s, axis=0, keepdims=True) for s in sums]
    lines += [high.astype(F32), low.astype(F32)]
    lines.append(jnp.zeros((16 - len(lines), LANES), F32))
    terms = jnp.concatenate(lines, axis=0).astype(BF16)
    for j in range(ctx):
        terms_ref[j] = terms


def local(q, k, v, c, short_taps, residues, rates):
    length, wide = q.shape
    taps = short_taps.shape[1]
    span = taps - 1
    groups, modes = residues.shape
    members = wide // groups
    ctx = lax.axis_size("ctx")
    tiles = wide // LANES
    per = LANES // members
    rows = length // BLOCK * members
    lanes = per * BLOCK
    sizes = (members, modes, taps, ctx)
    me = lax.axis_index("ctx").astype(jnp.int32).reshape(1)
    prior = lax.ppermute(
        jnp.concatenate([q[length - span :], k[length - span :], v[length - span :]], axis=0),
        "ctx", [(i, i + 1) for i in range(ctx - 1)],
    )
    after = lax.ppermute(
        jnp.concatenate([q[:span], k[:span], v[:span], c[:span]], axis=0),
        "ctx", [(i + 1, i) for i in range(ctx - 1)],
    )
    tap_rows = short_taps.reshape(3 * taps, wide)
    rate_col, res_col = rates.reshape(groups * modes, 1), residues.reshape(groups * modes, 1)
    rate_row = rates.reshape(tiles, 1, per * modes)
    res_row = residues.reshape(tiles, 1, per * modes)
    near = jnp.stack(
        [
            jnp.sum(residues, axis=1),
            jnp.sum(residues * jnp.exp(-rates), axis=1),
            jnp.sum(residues * jnp.exp(rates), axis=1),
        ]
    )
    near = jnp.repeat(near, members, axis=1)

    smem = pl.BlockSpec(memory_space=pltpu.SMEM)
    stream = pl.BlockSpec((length, LANES), lambda i: (0, i))
    col = pl.BlockSpec((per * modes, 1), lambda i: (i, 0))
    row = pl.BlockSpec((1, 1, per * modes), lambda i: (i, 0, 0))
    turned = pl.BlockSpec((rows, lanes), lambda i: (i, 0))
    ends = pl.BlockSpec((rows, per * modes), lambda i: (i, 0))
    swap = pl.BlockSpec((ctx, members, per * modes), lambda i: (0, i, 0))

    def strip(n):
        return pl.BlockSpec((n, LANES), lambda i: (0, i))

    turned_shape = jax.ShapeDtypeStruct((tiles * rows, lanes), BF16)
    ends_shape = jax.ShapeDtypeStruct((tiles * rows, per * modes), F32)
    x, h, ef, eb, send = pl.pallas_call(
        functools.partial(states_kernel, sizes),
        grid=(tiles,),
        in_specs=[smem, stream, stream, stream, stream, strip(3 * span), strip(3 * taps), col, row],
        out_specs=[turned, turned, ends, ends, swap],
        out_shape=[
            turned_shape, turned_shape, ends_shape, ends_shape,
            jax.ShapeDtypeStruct((ctx, tiles * members, per * modes), F32),
        ],
        scratch_shapes=[
            pltpu.VMEM((3, PAD + length, LANES), F32),
            pltpu.VMEM((length, LANES), BF16),
            pltpu.VMEM((length, LANES), BF16),
            pltpu.VMEM((2 * per * modes, lanes), BF16),
            pltpu.VMEM((2 * per * modes, lanes), BF16),
        ],
        cost_estimate=pl.CostEstimate(flops=4 * 10**9, bytes_accessed=26 * 10**6, transcendentals=0),
        name="states",
    )(me, q, k, v, c, prior, tap_rows, rate_col, rate_row)
    recv = lax.all_to_all(send, "ctx", split_axis=0, concat_axis=0, tiled=True)
    y, z, lag = pl.pallas_call(
        functools.partial(inner_kernel, sizes),
        grid=(tiles,),
        in_specs=[turned, turned, col, col],
        out_specs=[turned, turned, row],
        out_shape=[
            turned_shape, turned_shape, jax.ShapeDtypeStruct((tiles, 1, per * modes), F32),
        ],
        cost_estimate=pl.CostEstimate(flops=4 * 10**9, bytes_accessed=17 * 10**6, transcendentals=0),
        name="inner",
    )(x, h, rate_col, res_col)
    big = jax.ShapeDtypeStruct((length, wide), BF16)
    mixed, gq, gk, gv, terms = pl.pallas_call(
        functools.partial(finish_kernel, sizes),
        grid=(tiles,),
        in_specs=[
            smem, stream, stream, stream, stream, strip(3 * span), strip(4 * span), strip(3 * taps),
            row, row, row, turned, turned, ends, ends, swap, strip(3),
        ],
        out_specs=[
            stream, stream, stream, stream,
            pl.BlockSpec((ctx, 16, LANES), lambda i: (0, 0, i)),
        ],
        out_shape=[big, big, big, big, jax.ShapeDtypeStruct((ctx, 16, wide), BF16)],
        scratch_shapes=[
            pltpu.VMEM((3, 2 * PAD + length, LANES), F32),
            pltpu.VMEM((3, PAD + length, LANES), F32),
            pltpu.VMEM((length, LANES), BF16),
            pltpu.VMEM((length, LANES), BF16),
        ],
        cost_estimate=pl.CostEstimate(flops=8 * 10**9, bytes_accessed=42 * 10**6, transcendentals=0),
        name="finish",
    )(me, q, k, v, c, prior, after, tap_rows, rate_row, res_row, lag, y, z, ef, eb, recv, near)
    total = jnp.sum(
        lax.all_to_all(terms, "ctx", split_axis=0, concat_axis=0, tiled=True).astype(F32), axis=0
    )
    count = 3 * taps
    grad_taps = total[:count].reshape(3, taps, wide)
    grad_res = (total[count] + total[count + 1]).reshape(groups, modes)
    return mixed, gq, gk, gv, grad_taps, grad_res


def solution(mesh):
    stream = P("ctx", "tp")
    return jax.shard_map(
        local,
        mesh=mesh,
        in_specs=(stream, stream, stream, stream, P(None, None, "tp"), P("tp", None), P("tp", None)),
        out_specs=(stream, stream, stream, stream, P(None, None, "tp"), P("tp", None)),
        check_vma=False,
    )
```

```python
import functools
import jax
import jax.numpy as jnp
from jax import lax
from jax.experimental import pallas as pl
from jax.experimental.pallas import tpu as pltpu
from jax.sharding import PartitionSpec as P

F32 = jnp.float32
BF16 = jnp.bfloat16
BLOCK = 128
LANES = 128
TILES = 2
PAD = 8
PART = 64
KEPT = (0, 1, 2)


def dot(a, b, a_dim=1, b_dim=0, precision=None):
    return lax.dot_general(
        a, b, (((a_dim,), (b_dim,)), ((), ())), precision=precision, preferred_element_type=F32
    )


def iota(shape, axis):
    return lax.broadcasted_iota(jnp.int32, shape, axis)


def split(value):
    high = value.astype(BF16)
    return high, (value - high.astype(F32)).astype(BF16)


def mask(condition):
    return condition.astype(F32).astype(BF16)


def eye():
    shape = (BLOCK, BLOCK)
    return mask(iota(shape, 0) == iota(shape, 1))


def fine_dot(a, b, a_dim=1, b_dim=0):
    rows = a.shape[0]
    a_high, a_low = split(a)
    b_high, b_low = split(b)
    wide = dot(jnp.concatenate([a_high, a_low], axis=0), b_high, a_dim, b_dim)
    return wide[:rows] + (wide[rows:] + dot(a_high, b_low, a_dim, b_dim))


def as_row(value):
    groups, modes = value.shape
    width = groups * modes
    pick = mask(iota((modes, width), 1) % modes == iota((modes, width), 0))
    high = value.astype(BF16).astype(F32)
    middle = (value - high).astype(BF16).astype(F32)
    low = value - high - middle
    wide = dot(jnp.concatenate([high, middle, low], axis=0).astype(BF16), pick)
    own = iota((3 * groups, width), 1) // modes == iota((3 * groups, width), 0) % groups
    wide = jnp.where(own, wide, 0.0)
    parts = [
        jnp.sum(wide[i * groups : (i + 1) * groups], axis=0, keepdims=True) for i in range(3)
    ]
    return parts[0] + (parts[1] + parts[2])


def powers(rate_row, first, down):
    width = rate_row.shape[1]
    row = iota((8, width), 0).astype(F32)
    lag = 7.0 - row if down else row
    part = jnp.exp(-rate_row * (lag + first))
    factor = jnp.exp(-rate_row * 8.0)
    parts = [part]
    for _ in range(BLOCK // 8 - 1):
        parts.append(parts[-1] * factor)
    return jnp.concatenate(parts[::-1] if down else parts, axis=0)


def fill_streams(streams, prior_ref, us, length):
    span = prior_ref.shape[0] // len(streams)
    for i, ref in enumerate(streams):
        us[i, PAD - span : PAD, :] = prior_ref[i * span : (i + 1) * span, :].astype(F32)
        us[i, PAD : PAD + length, :] = ref[...].astype(F32)


def windows(us, i, start, rows, taps):
    return [us[i, PAD + start - j : PAD + start - j + rows, :] for j in range(taps)]


def short(taps_ref, i, wins):
    total = taps_ref[i, 0:1, :] * wins[0]
    for j in range(1, len(wins)):
        total = total + taps_ref[i, j : j + 1, :] * wins[j]
    return total


def states_tile(
    sizes, me, q_ref, k_ref, v_ref, c_ref, prior_ref, taps_ref, rates,
    x_ref, h_ref, ef_ref, eb_ref, send_ref, short_refs, us, gs, ls, af, ab,
):
    members, modes, taps, ctx = sizes
    length = q_ref.shape[0]
    count, groups = length // BLOCK, LANES // members
    width = groups * modes
    unit = eye()
    rate = as_row(rates)
    fill_streams((q_ref, k_ref, v_ref), prior_ref, us, length)
    half = BLOCK // 2
    for n in range(count):
        for part in range(2):
            start = n * BLOCK + part * half
            rows = slice(start, start + half)
            shorts = [short(taps_ref, i, windows(us, i, start, half, taps)) for i in range(3)]
            for i, ref in short_refs.items():
                ref[rows, :] = shorts[i].astype(BF16)
            gs[rows, :] = (shorts[1] * shorts[2]).astype(BF16)
            ls[rows, :] = (c_ref[rows, :].astype(F32) * shorts[0]).astype(BF16)
        if n % 2 == 0 and n + 1 < count:
            continue
        blocks = [n - 1, n] if n % 2 else [n]
        for source, target in ((gs, x_ref), (ls, h_ref)):
            rows = slice(blocks[0] * BLOCK, (n + 1) * BLOCK)
            turned = dot(unit, source[rows, :], 1, 1).astype(BF16)
            for at, m in enumerate(blocks):
                for g in range(groups):
                    target[m * members : (m + 1) * members, g * BLOCK : (g + 1) * BLOCK] = turned[
                        g * members : (g + 1) * members, at * BLOCK : (at + 1) * BLOCK
                    ]
        if n == 1:
            for table, array in ((af, powers(rate, 0.0, True)), (ab, powers(rate, 0.0, False))):
                both = jnp.concatenate(split(array), axis=1)
                lane_group = iota(both.shape, 1) % width // modes
                for g in range(groups):
                    table[g * BLOCK : (g + 1) * BLOCK, :] = both * mask(lane_group == g)
    decay = jnp.exp(-rate * float(BLOCK))
    forward = dot(x_ref[...], af[...])
    forward = forward[:, :width] + forward[:, width:]
    backward = dot(h_ref[...], ab[...])
    backward = backward[:, :width] + backward[:, width:]
    ef_ref[...] = forward
    eb_ref[...] = backward
    last = jnp.zeros((members, width), F32)
    first = jnp.zeros((members, width), F32)
    for n in range(count):
        m = count - 1 - n
        last = decay * last + forward[n * members : (n + 1) * members]
        first = decay * first + backward[m * members : (m + 1) * members]
    for j in range(ctx):
        send_ref[j] = jnp.where(j > me, last, first)


def states_kernel(sizes, *refs):
    members, modes, taps, ctx = sizes
    me_ref, q_ref, k_ref, v_ref, c_ref, prior_ref, taps_ref, rate_ref = refs[:8]
    x_ref, h_ref, ef_ref, eb_ref, send_ref = refs[8:13]
    kept = refs[13 : 13 + len(KEPT)]
    us, gs, ls, af, ab = refs[13 + len(KEPT) :]
    groups = LANES // members
    rows = x_ref.shape[0] // TILES
    for t in range(TILES):
        lanes, part = pl.ds(t * LANES, LANES), pl.ds(t * rows, rows)
        states_tile(
            sizes, me_ref[0],
            *[r.at[:, lanes] for r in (q_ref, k_ref, v_ref, c_ref, prior_ref)],
            taps_ref.at[:, :, lanes], rate_ref[t * groups : (t + 1) * groups, :],
            *[r.at[part, :] for r in (x_ref, h_ref, ef_ref, eb_ref)],
            send_ref.at[:, pl.ds(t * members, members), :],
            {i: r.at[:, lanes] for i, r in zip(KEPT, kept)},
            us.at[t], gs.at[t], ls.at[t], af.at[t], ab.at[t],
        )


def pairs_tile(sizes, x_ref, h_ref, rates, grad_ref):
    members, modes, taps, ctx = sizes
    groups = LANES // members
    width = groups * modes
    rate = as_row(rates)
    row, col = iota((BLOCK, BLOCK), 0), iota((BLOCK, BLOCK), 1)
    causal = row + col < BLOCK
    flip = mask(row + col == BLOCK - 1)
    sums = []
    for p in range(0, groups, 2):
        pair = range(p, min(p + 2, groups))
        stack = [h_ref[:, g * BLOCK : (g + 1) * BLOCK] for g in pair]
        turned = dot(flip, jnp.concatenate(stack, axis=0), 1, 1).astype(BF16)
        for at, g in enumerate(pair):
            x = x_ref[:, g * BLOCK : (g + 1) * BLOCK]
            rows = x.shape[0]
            pairs = jnp.where(causal, dot(turned[:, at * rows : (at + 1) * rows], x), 0.0)
            total = pairs[0:8]
            for i in range(1, BLOCK // 8):
                total = total + pltpu.roll(pairs[8 * i : 8 * i + 8], 8 * i, 1)
            sums.append(pltpu.roll(total, 0, 1, stride=1, stride_axis=0))
    crossed = fine_dot(jnp.concatenate(sums, axis=0), powers(rate, 0.0, True))
    shape = (8 * groups, width)
    grad_ref[...] = jnp.sum(
        jnp.where(iota(shape, 1) // modes == iota(shape, 0) // 8, crossed, 0.0), axis=0, keepdims=True
    )


def pairs_kernel(sizes, x_ref, h_ref, rate_ref, grad_ref):
    groups = LANES // sizes[0]
    rows = x_ref.shape[0] // TILES
    for t in range(TILES):
        part, own = pl.ds(t * rows, rows), slice(t * groups, (t + 1) * groups)
        pairs_tile(sizes, x_ref.at[part, :], h_ref.at[part, :], rate_ref[own, :], grad_ref.at[t])


def conv_steps(
    sizes, length, me, rates, residues, lag_ref, x_ref, h_ref, ef_ref, eb_ref, recv_ref,
    ts, rs, turn, note,
):
    members, modes, taps, ctx = sizes
    count, groups = length // BLOCK, LANES // members
    width = groups * modes
    rate, res = as_row(rates), as_row(residues)
    states, lefts, own = [], {}, {}

    def prepare():
        whole, decay = jnp.exp(-rate * float(length)), jnp.exp(-rate * float(BLOCK))
        ahead = jnp.zeros((members, width), F32)
        behind = jnp.zeros((members, width), F32)
        for i in range(ctx - 1):
            j = ctx - 1 - i
            ahead = jnp.where(i < me, whole * ahead + recv_ref[i], ahead)
            behind = jnp.where(j > me, whole * behind + recv_ref[j], behind)
        incoming = behind
        forward, backward = [], [None] * count
        for n in range(count):
            m = count - 1 - n
            forward.append(ahead)
            ahead = decay * ahead + ef_ref[n * members : (n + 1) * members, :]
            backward[m] = behind
            behind = decay * behind + eb_ref[m * members : (m + 1) * members, :]
        cross = forward[0] * eb_ref[0:members, :]
        for n in range(1, count):
            cross = cross + forward[n] * eb_ref[n * members : (n + 1) * members, :]
        states.extend((forward, backward))

        order = iota((PAD, width), 0).astype(F32)
        lane_group = iota((members, width), 1) // modes
        channel_own = iota((groups, LANES), 1) // members == iota((groups, LANES), 0)

        def spread(state):
            return jnp.concatenate(
                [jnp.where(lane_group == g, state, 0.0) for g in range(groups)], axis=0
            )

        def near(shift):
            sums = jnp.sum(residues * jnp.exp(-rates * shift), axis=1, keepdims=True)
            return jnp.sum(jnp.where(channel_own, sums, 0.0), axis=0, keepdims=True)

        note[0] = fine_dot(res * jnp.exp(-rate * (order + 1.0)), spread(ahead), 1, 1)
        note[1] = fine_dot(res * jnp.exp(rate * order), spread(incoming), 1, 1)
        note[2, 0:1, :] = near(0.0)
        note[2, 1:2, :] = near(1.0)
        note[2, 2:3, :] = near(-1.0)
        note[2, 3:4, :] = (
            jnp.exp(-rate) * jnp.sum(cross, axis=0, keepdims=True) + lag_ref[...]
        )

    def begin(d):
        down = d == 1
        mine = iota((groups, width), 1) // modes == iota((groups, width), 0)
        response = fine_dot(jnp.where(mine, res, 0.0), powers(rate, 0.0, down), 1, 1)
        high, low = split(jnp.transpose(res * powers(rate, 1.0, down)))
        state = jnp.concatenate(states[d], axis=0)
        wide = state.astype(BF16).astype(F32)
        fine = pltpu.roll(state - wide, 2 * modes, 1)
        again = pltpu.roll(wide, 4 * modes, 1)
        own[d] = (response, high, low, wide, fine, again)

    def group(d, g):
        down = d == 1
        response, high, low, wide, fine, again = own[d]
        square = (BLOCK, BLOCK)
        keep = iota(square, 1) <= iota(square, 0) if down else iota(square, 1) >= iota(square, 0)
        line = jnp.broadcast_to(response[g : g + 1], (8, BLOCK))
        line = pltpu.roll(line, int(down), 1, stride=1, stride_axis=0)
        parts = [line] + [pltpu.roll(line, 8 * i, 1) for i in range(1, BLOCK // 8)]
        ts[d, g] = jnp.concatenate(parts, axis=0).astype(BF16) * mask(keep)
        rows = slice(g * modes, (g + 1) * modes)
        for turns, piece in ((0, high), (1, high), (2, low)):
            at = (g * modes + 2 * modes * turns) % width
            rs[d, g, at : at + modes, :] = piece[rows]
        if g % 2 == 0:
            p = g // 2
            quarter = iota((count * members, width), 1) // (2 * modes)
            lefts[d] = jnp.where(
                quarter == p, wide, jnp.where(quarter == (p + 1) % 4, fine, again)
            ).astype(BF16)
        source = (x_ref, h_ref)[d]
        both = jnp.concatenate([source[:, g * BLOCK : (g + 1) * BLOCK], lefts[d]], axis=1)
        out = dot(both, jnp.concatenate([ts[d, g], rs[d, g]], axis=0))
        for n in range(count):
            turn[d, n, g * members : (g + 1) * members, :] = out[n * members : (n + 1) * members]

    steps = [prepare]
    for d in range(2):
        steps.append(functools.partial(begin, d))
        steps.extend(functools.partial(group, d, g) for g in range(groups))
    return steps


def turn_steps(length, turn, lo, gg):
    def step(n):
        rows = slice(n * BLOCK, (n + 1) * BLOCK)
        lo[rows, :] = jnp.transpose(turn[0, n])
        gg[rows, :] = jnp.transpose(turn[1, n])

    return [functools.partial(step, n) for n in reversed(range(length // BLOCK))]


def output_steps(
    sizes, q_ref, k_ref, v_ref, c_ref, prior_ref, after_ref, taps_ref, short_refs,
    mixed_ref, gq_ref, gk_ref, gv_ref, terms_ref, us, es, note, lo, gg,
):
    members, modes, taps, ctx = sizes
    length = q_ref.shape[0]
    count = length // BLOCK
    span = taps - 1
    streams = (q_ref, k_ref, v_ref)
    part = PART
    ones = jnp.ones((8, BLOCK), BF16)
    sums = [jnp.zeros((8, LANES), F32) for _ in range(3 * taps)]

    def prepare():
        head = after_ref[...].astype(F32)
        rest = jnp.zeros((PAD - span, LANES), F32)
        ends = []
        for i in range(3):
            if i in short_refs:
                us[i, PAD + length - span : PAD + length, :] = streams[i][
                    length - span :, :
                ].astype(F32)
            else:
                us[i, PAD - span : PAD, :] = prior_ref[i * span : (i + 1) * span, :].astype(F32)
                us[i, PAD : PAD + length, :] = streams[i][...].astype(F32)
            us[i, PAD + length : 2 * PAD + length, :] = jnp.concatenate(
                [head[i * span : (i + 1) * span], rest], axis=0
            )
            ends.append(short(taps_ref, i, windows(us, i, length, PAD, taps)))
        query, key, value = ends
        cot = jnp.concatenate([head[3 * span : 4 * span], rest], axis=0)
        line = jnp.zeros((1, LANES), F32)
        second = iota((PAD, LANES), 0) == 1
        gated = (key * value).astype(BF16).astype(F32)
        grad_long = (cot * query).astype(BF16).astype(F32)
        gated_prev = jnp.where(second, jnp.concatenate([line, gated[:-1]], axis=0), 0.0)
        grad_prev = jnp.where(second, jnp.concatenate([line, grad_long[:-1]], axis=0), 0.0)
        out = note[0] + note[2, 0:1, :] * gated + note[2, 1:2, :] * gated_prev
        back = note[1] - note[2, 2:3, :] * grad_prev
        for i, edge in enumerate((cot * out, back * value, back * key)):
            es[i, length : length + PAD, :] = edge

    def tap(i, j):
        return jnp.broadcast_to(taps_ref[i, j : j + 1, :], (16, LANES)).astype(BF16)

    def scale(value, row):
        return (value.reshape(value.shape[0] // 16, 16, LANES) * row[None]).reshape(value.shape)

    tap_rows = [[tap(i, j) for j in range(taps)] for i in range(3)]

    def block(n):
        products = [[] for _ in range(3 * taps)]
        for start in reversed(range(n * BLOCK, (n + 1) * BLOCK, part)):
            rows = slice(start, start + part)
            long_out, grad_gated = lo[rows, :], gg[rows, :]
            key, value = [short_refs[i][rows, :].astype(F32) for i in (1, 2)]
            mixed_ref[rows, :] = short_refs[0][rows, :] * long_out.astype(BF16)
            edges = (c_ref[rows, :].astype(F32) * long_out, grad_gated * value, grad_gated * key)
            for i, (edge, target) in enumerate(zip(edges, (gq_ref, gk_ref, gv_ref))):
                es[i, rows, :] = edge
                stream = streams[i][rows, :]
                total = None
                for j in range(taps):
                    later = (es[i, start + j : start + j + part, :] if j else edge).astype(BF16)
                    products[i * taps + j].insert(0, later * stream)
                    term = scale(later, tap_rows[i][j])
                    total = term if total is None else total + term
                target[rows, :] = total
        for a in range(0, 3 * taps, 2):
            wide = [jnp.concatenate(p, axis=0) for p in products[a : a + 2]]
            added = dot(ones, jnp.concatenate(wide, axis=1))
            for at in range(len(wide)):
                sums[a + at] = sums[a + at] + added[:, at * LANES : (at + 1) * LANES]

    def end():
        high, low = split(note[2, 3:4, :])
        lines = [s[0:1] for s in sums] + [high.astype(F32), low.astype(F32)]
        lines.append(jnp.zeros((16 - len(lines), LANES), F32))
        terms = jnp.concatenate(lines, axis=0).astype(BF16)
        for j in range(ctx):
            terms_ref[j] = terms

    blocks = [functools.partial(block, n) for n in reversed(range(count))]
    return prepare, blocks, end


def finish_kernel(sizes, *refs):
    members = sizes[0]
    me_ref, q_ref, k_ref, v_ref, c_ref, prior_ref, after_ref, taps_ref, rate_ref, res_ref = refs[:10]
    lag_ref, x_ref, h_ref, ef_ref, eb_ref, recv_ref = refs[10:16]
    kept, rest = refs[16 : 16 + len(KEPT)], refs[16 + len(KEPT) :]
    mixed_ref, gq_ref, gk_ref, gv_ref, terms_ref, us, es, ts, rs, turn, note, lo, gg = rest
    length = q_ref.shape[0]
    groups = LANES // members
    rows = x_ref.shape[0] // TILES
    step, last = pl.program_id(0), pl.num_programs(0) - 1

    def convolve(t):
        part, own = pl.ds(t * rows, rows), slice(t * groups, (t + 1) * groups)
        return conv_steps(
            sizes, length, me_ref[0], rate_ref[own, :], res_ref[own, :], lag_ref.at[t],
            *[r.at[part, :] for r in (x_ref, h_ref, ef_ref, eb_ref)],
            recv_ref.at[:, pl.ds(t * members, members), :],
            ts.at[t], rs.at[t], turn.at[t], note.at[1, t],
        )

    def output(t):
        lanes = pl.ds(t * LANES, LANES)
        return output_steps(
            sizes, *[r.at[:, lanes] for r in (q_ref, k_ref, v_ref, c_ref, prior_ref, after_ref)],
            taps_ref.at[:, :, lanes], {i: r.at[:, lanes] for i, r in zip(KEPT, kept)},
            *[r.at[:, lanes] for r in (mixed_ref, gq_ref, gk_ref, gv_ref)],
            terms_ref.at[:, :, lanes], us.at[t], es.at[t], note.at[0, t], lo.at[t], gg.at[t],
        )

    def settle(t):
        note[0, t] = note[1, t]

    @pl.when(step == 0)
    def _():
        rs[...] = jnp.zeros_like(rs)
        for t in range(TILES):
            for run in convolve(t) + turn_steps(length, turn.at[t], lo.at[t], gg.at[t]):
                run()
            settle(t)

    @pl.when((step > 0) & (step < last))
    def _():
        for t in range(TILES):
            prepare, blocks, end = output(t)
            work = convolve(t)
            turns = turn_steps(length, turn.at[t], lo.at[t], gg.at[t])
            early = (len(blocks) + 1) // 2
            share = -(-len(work) // early)
            prepare()
            ready = 0
            for k, block in enumerate(blocks):
                for run in work[k * share : (k + 1) * share]:
                    run()
                block()
                if (k + 1) * share >= len(work):
                    while ready <= k and ready < (k + 1 - early) * 2 + 2:
                        turns[ready]()
                        ready += 1
            for run in turns[ready:]:
                run()
            end()
            settle(t)

    @pl.when(step == last)
    def _():
        for t in range(TILES):
            prepare, blocks, end = output(t)
            for run in [prepare] + blocks + [end]:
                run()


def local(q, k, v, c, short_taps, residues, rates):
    length, wide = q.shape
    taps = short_taps.shape[1]
    span = taps - 1
    groups, modes = residues.shape
    members = wide // groups
    ctx = lax.axis_size("ctx")
    tiles = wide // LANES
    per = LANES // members
    width = per * modes
    rows = length // BLOCK * members
    lanes = per * BLOCK
    sizes = (members, modes, taps, ctx)
    me = lax.axis_index("ctx").astype(jnp.int32).reshape(1)
    prior = lax.ppermute(
        jnp.concatenate([q[length - span :], k[length - span :], v[length - span :]], axis=0),
        "ctx", [(i, i + 1) for i in range(ctx - 1)],
    )
    after = lax.ppermute(
        jnp.concatenate([q[:span], k[:span], v[:span], c[:span]], axis=0),
        "ctx", [(i + 1, i) for i in range(ctx - 1)],
    )

    smem = pl.BlockSpec(memory_space=pltpu.SMEM)
    stream = pl.BlockSpec((length, TILES * LANES), lambda i: (0, i))
    tap_spec = pl.BlockSpec((3, taps, TILES * LANES), lambda i: (0, 0, i))
    group_spec = pl.BlockSpec((TILES * per, modes), lambda i: (i, 0))
    row = pl.BlockSpec((TILES, 1, width), lambda i: (i, 0, 0))
    turned = pl.BlockSpec((TILES * rows, lanes), lambda i: (i, 0))
    ends = pl.BlockSpec((TILES * rows, width), lambda i: (i, 0))
    swap = pl.BlockSpec((ctx, TILES * members, width), lambda i: (0, i, 0))

    def strip(n):
        return pl.BlockSpec((n, TILES * LANES), lambda i: (0, i))

    turned_shape = jax.ShapeDtypeStruct((tiles * rows, lanes), BF16)
    ends_shape = jax.ShapeDtypeStruct((tiles * rows, width), F32)
    big = jax.ShapeDtypeStruct((length, wide), BF16)
    x, h, ef, eb, send, *kept = pl.pallas_call(
        functools.partial(states_kernel, sizes),
        grid=(tiles // TILES,),
        in_specs=[smem, stream, stream, stream, stream, strip(3 * span), tap_spec, group_spec],
        out_specs=[turned, turned, ends, ends, swap] + [stream] * len(KEPT),
        out_shape=[
            turned_shape, turned_shape, ends_shape, ends_shape,
            jax.ShapeDtypeStruct((ctx, tiles * members, width), F32),
        ] + [big] * len(KEPT),
        scratch_shapes=[
            pltpu.VMEM((TILES, 3, PAD + length, LANES), F32),
            pltpu.VMEM((TILES, length, LANES), BF16),
            pltpu.VMEM((TILES, length, LANES), BF16),
            pltpu.VMEM((TILES, lanes, 2 * width), BF16),
            pltpu.VMEM((TILES, lanes, 2 * width), BF16),
        ],
        cost_estimate=pl.CostEstimate(flops=4 * 10**9, bytes_accessed=34 * 10**6, transcendentals=0),
        name="states",
    )(me, q, k, v, c, prior, short_taps, rates)
    recv = lax.all_to_all(send, "ctx", split_axis=0, concat_axis=0, tiled=True)
    lag = pl.pallas_call(
        functools.partial(pairs_kernel, sizes),
        grid=(tiles // TILES,),
        in_specs=[turned, turned, group_spec],
        out_specs=row,
        out_shape=jax.ShapeDtypeStruct((tiles, 1, width), F32),
        cost_estimate=pl.CostEstimate(flops=4 * 10**9, bytes_accessed=17 * 10**6, transcendentals=0),
        name="pairs",
    )(x, h, rates)
    steps = tiles // TILES

    def late(spec):
        return pl.BlockSpec(spec.block_shape, lambda i: spec.index_map(jnp.maximum(i - 1, 0)))

    def soon(spec):
        return pl.BlockSpec(spec.block_shape, lambda i: spec.index_map(jnp.minimum(i, steps - 1)))

    lines = late(stream)
    mixed, gq, gk, gv, terms = pl.pallas_call(
        functools.partial(finish_kernel, sizes),
        grid=(steps + 1,),
        in_specs=[
            smem, lines, lines, lines, lines, late(strip(3 * span)), late(strip(4 * span)),
            late(tap_spec), soon(group_spec), soon(group_spec), soon(row), soon(turned),
            soon(turned), soon(ends), soon(ends), soon(swap),
        ] + [lines] * len(KEPT),
        out_specs=[
            lines, lines, lines, lines,
            late(pl.BlockSpec((ctx, 16, TILES * LANES), lambda i: (0, 0, i))),
        ],
        out_shape=[big, big, big, big, jax.ShapeDtypeStruct((ctx, 16, wide), BF16)],
        scratch_shapes=[
            pltpu.VMEM((TILES, 3, 2 * PAD + length, LANES), F32),
            pltpu.VMEM((TILES, 3, PAD + length, LANES), F32),
            pltpu.VMEM((TILES, 2, per, BLOCK, BLOCK), BF16),
            pltpu.VMEM((TILES, 2, per, width, BLOCK), BF16),
            pltpu.VMEM((TILES, 2, length // BLOCK, LANES, BLOCK), F32),
            pltpu.VMEM((2, TILES, 3, PAD, LANES), F32),
            pltpu.VMEM((TILES, length, LANES), F32),
            pltpu.VMEM((TILES, length, LANES), F32),
        ],
        cost_estimate=pl.CostEstimate(flops=8 * 10**9, bytes_accessed=50 * 10**6, transcendentals=0),
        name="finish",
    )(me, q, k, v, c, prior, after, short_taps, rates, residues, lag, x, h, ef, eb, recv, *kept)
    total = jnp.sum(
        lax.all_to_all(terms, "ctx", split_axis=0, concat_axis=0, tiled=True).astype(F32), axis=0
    )
    count = 3 * taps
    grad_taps = total[:count].reshape(3, taps, wide)
    grad_res = (total[count] + total[count + 1]).reshape(groups, modes)
    return mixed, gq, gk, gv, grad_taps, grad_res


def solution(mesh):
    stream = P("ctx", "tp")
    return jax.shard_map(
        local,
        mesh=mesh,
        in_specs=(stream, stream, stream, stream, P(None, None, "tp"), P("tp", None), P("tp", None)),
        out_specs=(stream, stream, stream, stream, P(None, None, "tp"), P("tp", None)),
        check_vma=False,
    )
```

```python
import functools
import jax
import jax.numpy as jnp
from jax import lax
from jax.experimental import pallas as pl
from jax.experimental.pallas import tpu as pltpu
from jax.sharding import PartitionSpec as P

F32 = jnp.float32
BF16 = jnp.bfloat16
BLOCK = 128
LANES = 128
TILES = 2
PAD = 8
PART = 64
KEPT = (0, 1, 2)


def dot(a, b, a_dim=1, b_dim=0, precision=None):
    return lax.dot_general(
        a, b, (((a_dim,), (b_dim,)), ((), ())), precision=precision, preferred_element_type=F32
    )


def iota(shape, axis):
    return lax.broadcasted_iota(jnp.int32, shape, axis)


def split(value):
    high = value.astype(BF16)
    return high, (value - high.astype(F32)).astype(BF16)


def mask(condition):
    return condition.astype(F32).astype(BF16)


def eye():
    shape = (BLOCK, BLOCK)
    return mask(iota(shape, 0) == iota(shape, 1))


def fine_dot(a, b, a_dim=1, b_dim=0):
    rows = a.shape[0]
    a_high, a_low = split(a)
    b_high, b_low = split(b)
    wide = dot(jnp.concatenate([a_high, a_low], axis=0), b_high, a_dim, b_dim)
    return wide[:rows] + (wide[rows:] + dot(a_high, b_low, a_dim, b_dim))


def as_row(value):
    groups, modes = value.shape
    width = groups * modes
    pick = mask(iota((modes, width), 1) % modes == iota((modes, width), 0))
    high = value.astype(BF16).astype(F32)
    middle = (value - high).astype(BF16).astype(F32)
    low = value - high - middle
    wide = dot(jnp.concatenate([high, middle, low], axis=0).astype(BF16), pick)
    own = iota((3 * groups, width), 1) // modes == iota((3 * groups, width), 0) % groups
    wide = jnp.where(own, wide, 0.0)
    parts = [
        jnp.sum(wide[i * groups : (i + 1) * groups], axis=0, keepdims=True) for i in range(3)
    ]
    return parts[0] + (parts[1] + parts[2])


def powers(rate_row, first, down):
    width = rate_row.shape[1]
    row = iota((8, width), 0).astype(F32)
    lag = 7.0 - row if down else row
    part = jnp.exp(-rate_row * (lag + first))
    factor = jnp.exp(-rate_row * 8.0)
    parts = [part]
    for _ in range(BLOCK // 8 - 1):
        parts.append(parts[-1] * factor)
    return jnp.concatenate(parts[::-1] if down else parts, axis=0)


def fill_streams(streams, prior_ref, us, length):
    span = prior_ref.shape[0] // len(streams)
    for i, ref in enumerate(streams):
        us[i, PAD - span : PAD, :] = prior_ref[i * span : (i + 1) * span, :].astype(F32)
        us[i, PAD : PAD + length, :] = ref[...].astype(F32)


def windows(us, i, start, rows, taps):
    return [us[i, PAD + start - j : PAD + start - j + rows, :] for j in range(taps)]


def short(taps_ref, i, wins):
    total = taps_ref[i, 0:1, :] * wins[0]
    for j in range(1, len(wins)):
        total = total + taps_ref[i, j : j + 1, :] * wins[j]
    return total


def states_tile(
    sizes, me, q_ref, k_ref, v_ref, c_ref, prior_ref, taps_ref, rates,
    x_ref, h_ref, ef_ref, eb_ref, send_ref, short_refs, us, gs, ls, af, ab,
):
    members, modes, taps, ctx = sizes
    length = q_ref.shape[0]
    count, groups = length // BLOCK, LANES // members
    width = groups * modes
    unit = eye()
    rate = as_row(rates)
    fill_streams((q_ref, k_ref, v_ref), prior_ref, us, length)
    half = BLOCK // 2
    for n in range(count):
        for part in range(2):
            start = n * BLOCK + part * half
            rows = slice(start, start + half)
            shorts = [short(taps_ref, i, windows(us, i, start, half, taps)) for i in range(3)]
            for i, ref in short_refs.items():
                ref[rows, :] = shorts[i].astype(BF16)
            gs[rows, :] = (shorts[1] * shorts[2]).astype(BF16)
            ls[rows, :] = (c_ref[rows, :].astype(F32) * shorts[0]).astype(BF16)
        if n % 2 == 0 and n + 1 < count:
            continue
        blocks = [n - 1, n] if n % 2 else [n]
        for source, target in ((gs, x_ref), (ls, h_ref)):
            rows = slice(blocks[0] * BLOCK, (n + 1) * BLOCK)
            turned = dot(unit, source[rows, :], 1, 1).astype(BF16)
            for at, m in enumerate(blocks):
                for g in range(groups):
                    target[m * members : (m + 1) * members, g * BLOCK : (g + 1) * BLOCK] = turned[
                        g * members : (g + 1) * members, at * BLOCK : (at + 1) * BLOCK
                    ]
        if n == 1:
            for table, array in ((af, powers(rate, 0.0, True)), (ab, powers(rate, 0.0, False))):
                both = jnp.concatenate(split(array), axis=1)
                lane_group = iota(both.shape, 1) % width // modes
                for g in range(groups):
                    table[g * BLOCK : (g + 1) * BLOCK, :] = both * mask(lane_group == g)
    decay = jnp.exp(-rate * float(BLOCK))
    forward = dot(x_ref[...], af[...])
    forward = forward[:, :width] + forward[:, width:]
    backward = dot(h_ref[...], ab[...])
    backward = backward[:, :width] + backward[:, width:]
    ef_ref[...] = forward
    eb_ref[...] = backward
    last = jnp.zeros((members, width), F32)
    first = jnp.zeros((members, width), F32)
    for n in range(count):
        m = count - 1 - n
        last = decay * last + forward[n * members : (n + 1) * members]
        first = decay * first + backward[m * members : (m + 1) * members]
    for j in range(ctx):
        send_ref[j] = jnp.where(j > me, last, first)


def states_kernel(sizes, *refs):
    members, modes, taps, ctx = sizes
    me_ref, q_ref, k_ref, v_ref, c_ref, prior_ref, taps_ref, rate_ref = refs[:8]
    x_ref, h_ref, ef_ref, eb_ref, send_ref = refs[8:13]
    kept = refs[13 : 13 + len(KEPT)]
    us, gs, ls, af, ab = refs[13 + len(KEPT) :]
    groups = LANES // members
    rows = x_ref.shape[0] // TILES
    for t in range(TILES):
        lanes, part = pl.ds(t * LANES, LANES), pl.ds(t * rows, rows)
        states_tile(
            sizes, me_ref[0],
            *[r.at[:, lanes] for r in (q_ref, k_ref, v_ref, c_ref, prior_ref)],
            taps_ref.at[:, :, lanes], rate_ref[t * groups : (t + 1) * groups, :],
            *[r.at[part, :] for r in (x_ref, h_ref, ef_ref, eb_ref)],
            send_ref.at[:, pl.ds(t * members, members), :],
            {i: r.at[:, lanes] for i, r in zip(KEPT, kept)},
            us.at[t], gs.at[t], ls.at[t], af.at[t], ab.at[t],
        )


def pairs_tile(sizes, x_ref, h_ref, rates, grad_ref):
    members, modes, taps, ctx = sizes
    groups = LANES // members
    width = groups * modes
    rate = as_row(rates)
    row, col = iota((BLOCK, BLOCK), 0), iota((BLOCK, BLOCK), 1)
    causal = row + col < BLOCK
    flip = mask(row + col == BLOCK - 1)
    sums = []
    for p in range(0, groups, 2):
        pair = range(p, min(p + 2, groups))
        stack = [h_ref[:, g * BLOCK : (g + 1) * BLOCK] for g in pair]
        turned = dot(flip, jnp.concatenate(stack, axis=0), 1, 1).astype(BF16)
        for at, g in enumerate(pair):
            x = x_ref[:, g * BLOCK : (g + 1) * BLOCK]
            rows = x.shape[0]
            pairs = jnp.where(causal, dot(turned[:, at * rows : (at + 1) * rows], x), 0.0)
            total = pairs[0:8]
            for i in range(1, BLOCK // 8):
                total = total + pltpu.roll(pairs[8 * i : 8 * i + 8], 8 * i, 1)
            sums.append(pltpu.roll(total, 0, 1, stride=1, stride_axis=0))
    crossed = fine_dot(jnp.concatenate(sums, axis=0), powers(rate, 0.0, True))
    shape = (8 * groups, width)
    grad_ref[...] = jnp.sum(
        jnp.where(iota(shape, 1) // modes == iota(shape, 0) // 8, crossed, 0.0), axis=0, keepdims=True
    )


def pairs_kernel(sizes, x_ref, h_ref, rate_ref, grad_ref):
    groups = LANES // sizes[0]
    rows = x_ref.shape[0] // TILES
    for t in range(TILES):
        part, own = pl.ds(t * rows, rows), slice(t * groups, (t + 1) * groups)
        pairs_tile(sizes, x_ref.at[part, :], h_ref.at[part, :], rate_ref[own, :], grad_ref.at[t])


def conv_steps(
    sizes, length, me, rates, residues, lag_ref, x_ref, h_ref, ef_ref, eb_ref, recv_ref,
    ts, rs, turn, note,
):
    members, modes, taps, ctx = sizes
    count, groups = length // BLOCK, LANES // members
    width = groups * modes
    rate, res = as_row(rates), as_row(residues)
    states, lefts, own = [], {}, {}

    def prepare():
        whole, decay = jnp.exp(-rate * float(length)), jnp.exp(-rate * float(BLOCK))
        ahead = jnp.zeros((members, width), F32)
        behind = jnp.zeros((members, width), F32)
        for i in range(ctx - 1):
            j = ctx - 1 - i
            ahead = jnp.where(i < me, whole * ahead + recv_ref[i], ahead)
            behind = jnp.where(j > me, whole * behind + recv_ref[j], behind)
        incoming = behind
        forward, backward = [], [None] * count
        for n in range(count):
            m = count - 1 - n
            forward.append(ahead)
            ahead = decay * ahead + ef_ref[n * members : (n + 1) * members, :]
            backward[m] = behind
            behind = decay * behind + eb_ref[m * members : (m + 1) * members, :]
        cross = forward[0] * eb_ref[0:members, :]
        for n in range(1, count):
            cross = cross + forward[n] * eb_ref[n * members : (n + 1) * members, :]
        states.extend((forward, backward))

        order = iota((PAD, width), 0).astype(F32)
        lane_group = iota((members, width), 1) // modes
        channel_own = iota((groups, LANES), 1) // members == iota((groups, LANES), 0)

        def spread(state):
            return jnp.concatenate(
                [jnp.where(lane_group == g, state, 0.0) for g in range(groups)], axis=0
            )

        def near(shift):
            sums = jnp.sum(residues * jnp.exp(-rates * shift), axis=1, keepdims=True)
            return jnp.sum(jnp.where(channel_own, sums, 0.0), axis=0, keepdims=True)

        note[0] = fine_dot(res * jnp.exp(-rate * (order + 1.0)), spread(ahead), 1, 1)
        note[1] = fine_dot(res * jnp.exp(rate * order), spread(incoming), 1, 1)
        note[2, 0:1, :] = near(0.0)
        note[2, 1:2, :] = near(1.0)
        note[2, 2:3, :] = near(-1.0)
        note[2, 3:4, :] = (
            jnp.exp(-rate) * jnp.sum(cross, axis=0, keepdims=True) + lag_ref[...]
        )

    def begin(d):
        down = d == 1
        mine = iota((groups, width), 1) // modes == iota((groups, width), 0)
        response = fine_dot(jnp.where(mine, res, 0.0), powers(rate, 0.0, down), 1, 1)
        high, low = split(jnp.transpose(res * powers(rate, 1.0, down)))
        state = jnp.concatenate(states[d], axis=0)
        wide = state.astype(BF16).astype(F32)
        fine = pltpu.roll(state - wide, 2 * modes, 1)
        again = pltpu.roll(wide, 4 * modes, 1)
        own[d] = (response, high, low, wide, fine, again)

    def group(d, g):
        down = d == 1
        response, high, low, wide, fine, again = own[d]
        square = (BLOCK, BLOCK)
        keep = iota(square, 1) <= iota(square, 0) if down else iota(square, 1) >= iota(square, 0)
        line = jnp.broadcast_to(response[g : g + 1], (8, BLOCK))
        line = pltpu.roll(line, int(down), 1, stride=1, stride_axis=0)
        parts = [line] + [pltpu.roll(line, 8 * i, 1) for i in range(1, BLOCK // 8)]
        ts[d, g] = jnp.concatenate(parts, axis=0).astype(BF16) * mask(keep)
        rows = slice(g * modes, (g + 1) * modes)
        for turns, piece in ((0, high), (1, high), (2, low)):
            at = (g * modes + 2 * modes * turns) % width
            rs[d, g, at : at + modes, :] = piece[rows]
        if g % 2 == 0:
            p = g // 2
            quarter = iota((count * members, width), 1) // (2 * modes)
            lefts[d] = jnp.where(
                quarter == p, wide, jnp.where(quarter == (p + 1) % 4, fine, again)
            ).astype(BF16)
        source = (x_ref, h_ref)[d]
        both = jnp.concatenate([source[:, g * BLOCK : (g + 1) * BLOCK], lefts[d]], axis=1)
        out = dot(both, jnp.concatenate([ts[d, g], rs[d, g]], axis=0))
        for n in range(count):
            turn[d, n, g * members : (g + 1) * members, :] = out[n * members : (n + 1) * members]

    steps = [prepare]
    for d in range(2):
        steps.append(functools.partial(begin, d))
        steps.extend(functools.partial(group, d, g) for g in range(groups))
    return steps


def turn_steps(length, turn, lo, gg):
    def step(n):
        rows = slice(n * BLOCK, (n + 1) * BLOCK)
        lo[rows, :] = jnp.transpose(turn[0, n])
        gg[rows, :] = jnp.transpose(turn[1, n])

    return [functools.partial(step, n) for n in reversed(range(length // BLOCK))]


def output_steps(
    sizes, q_ref, k_ref, v_ref, c_ref, prior_ref, after_ref, taps_ref, short_refs,
    mixed_ref, gq_ref, gk_ref, gv_ref, terms_ref, us, es, note, lo, gg,
):
    members, modes, taps, ctx = sizes
    length = q_ref.shape[0]
    count = length // BLOCK
    span = taps - 1
    streams = (q_ref, k_ref, v_ref)
    part = PART
    ones = jnp.ones((8, BLOCK), BF16)
    sums = [jnp.zeros((8, LANES), F32) for _ in range(3 * taps)]

    def prepare():
        head = after_ref[...].astype(F32)
        rest = jnp.zeros((PAD - span, LANES), F32)
        ends = []
        for i in range(3):
            if i in short_refs:
                us[i, PAD + length - span : PAD + length, :] = streams[i][
                    length - span :, :
                ].astype(F32)
            else:
                us[i, PAD - span : PAD, :] = prior_ref[i * span : (i + 1) * span, :].astype(F32)
                us[i, PAD : PAD + length, :] = streams[i][...].astype(F32)
            us[i, PAD + length : 2 * PAD + length, :] = jnp.concatenate(
                [head[i * span : (i + 1) * span], rest], axis=0
            )
            ends.append(short(taps_ref, i, windows(us, i, length, PAD, taps)))
        query, key, value = ends
        cot = jnp.concatenate([head[3 * span : 4 * span], rest], axis=0)
        line = jnp.zeros((1, LANES), F32)
        second = iota((PAD, LANES), 0) == 1
        gated = (key * value).astype(BF16).astype(F32)
        grad_long = (cot * query).astype(BF16).astype(F32)
        gated_prev = jnp.where(second, jnp.concatenate([line, gated[:-1]], axis=0), 0.0)
        grad_prev = jnp.where(second, jnp.concatenate([line, grad_long[:-1]], axis=0), 0.0)
        out = note[0] + note[2, 0:1, :] * gated + note[2, 1:2, :] * gated_prev
        back = note[1] - note[2, 2:3, :] * grad_prev
        for i, edge in enumerate((cot * out, back * value, back * key)):
            es[i, length : length + PAD, :] = edge

    def tap(i, j):
        return jnp.broadcast_to(taps_ref[i, j : j + 1, :], (16, LANES)).astype(BF16)

    def scale(value, row):
        return (value.reshape(value.shape[0] // 16, 16, LANES) * row[None]).reshape(value.shape)

    tap_rows = [[tap(i, j) for j in range(taps)] for i in range(3)]

    def block(n):
        products = [[] for _ in range(3 * taps)]
        for start in reversed(range(n * BLOCK, (n + 1) * BLOCK, part)):
            rows = slice(start, start + part)
            long_out, grad_gated = lo[rows, :], gg[rows, :]
            key, value = [short_refs[i][rows, :].astype(F32) for i in (1, 2)]
            mixed_ref[rows, :] = short_refs[0][rows, :] * long_out.astype(BF16)
            edges = (c_ref[rows, :].astype(F32) * long_out, grad_gated * value, grad_gated * key)
            for i, (edge, target) in enumerate(zip(edges, (gq_ref, gk_ref, gv_ref))):
                es[i, rows, :] = edge
                stream = streams[i][rows, :]
                total = None
                for j in range(taps):
                    later = (es[i, start + j : start + j + part, :] if j else edge).astype(BF16)
                    products[i * taps + j].insert(0, later * stream)
                    term = scale(later, tap_rows[i][j])
                    total = term if total is None else total + term
                target[rows, :] = total
        for a in range(0, 3 * taps, 2):
            wide = [jnp.concatenate(p, axis=0) for p in products[a : a + 2]]
            added = dot(ones, jnp.concatenate(wide, axis=1))
            for at in range(len(wide)):
                sums[a + at] = sums[a + at] + added[:, at * LANES : (at + 1) * LANES]

    def end():
        high, low = split(note[2, 3:4, :])
        lines = [s[0:1] for s in sums] + [high.astype(F32), low.astype(F32)]
        lines.append(jnp.zeros((16 - len(lines), LANES), F32))
        terms = jnp.concatenate(lines, axis=0).astype(BF16)
        for j in range(ctx):
            terms_ref[j] = terms

    blocks = [functools.partial(block, n) for n in reversed(range(count))]
    return prepare, blocks, end


def finish_kernel(sizes, *refs):
    members = sizes[0]
    me_ref, q_ref, k_ref, v_ref, c_ref, prior_ref, after_ref, taps_ref, rate_ref, res_ref = refs[:10]
    lag_ref, x_ref, h_ref, ef_ref, eb_ref, recv_ref = refs[10:16]
    kept, rest = refs[16 : 16 + len(KEPT)], refs[16 + len(KEPT) :]
    mixed_ref, gq_ref, gk_ref, gv_ref, terms_ref, us, es, ts, rs, turn, note, lo, gg = rest
    length = q_ref.shape[0]
    groups = LANES // members
    rows = x_ref.shape[0] // TILES
    step, last = pl.program_id(0), pl.num_programs(0) - 1

    def convolve(t):
        part, own = pl.ds(t * rows, rows), slice(t * groups, (t + 1) * groups)
        return conv_steps(
            sizes, length, me_ref[0], rate_ref[own, :], res_ref[own, :], lag_ref.at[t],
            *[r.at[part, :] for r in (x_ref, h_ref, ef_ref, eb_ref)],
            recv_ref.at[:, pl.ds(t * members, members), :],
            ts.at[t], rs.at[t], turn.at[t], note.at[1, t],
        )

    def output(t):
        lanes = pl.ds(t * LANES, LANES)
        return output_steps(
            sizes, *[r.at[:, lanes] for r in (q_ref, k_ref, v_ref, c_ref, prior_ref, after_ref)],
            taps_ref.at[:, :, lanes], {i: r.at[:, lanes] for i, r in zip(KEPT, kept)},
            *[r.at[:, lanes] for r in (mixed_ref, gq_ref, gk_ref, gv_ref)],
            terms_ref.at[:, :, lanes], us.at[t], es.at[t], note.at[0, t], lo.at[t], gg.at[t],
        )

    def settle(t):
        note[0, t] = note[1, t]

    @pl.when(step == 0)
    def _():
        rs[...] = jnp.zeros_like(rs)
        for t in range(TILES):
            for run in convolve(t) + turn_steps(length, turn.at[t], lo.at[t], gg.at[t]):
                run()
            settle(t)

    @pl.when((step > 0) & (step < last))
    def _():
        for t in range(TILES):
            prepare, blocks, end = output(t)
            work = convolve(t)
            turns = turn_steps(length, turn.at[t], lo.at[t], gg.at[t])
            early = len(blocks)
            share = -(-len(work) // early)
            prepare()
            ready = 0
            for k, block in enumerate(blocks):
                for run in work[k * share : (k + 1) * share]:
                    run()
                block()
                if (k + 1) * share >= len(work):
                    while ready <= k and ready < (k + 1 - early) * 2 + 2:
                        turns[ready]()
                        ready += 1
            for run in turns[ready:]:
                run()
            end()
            settle(t)

    @pl.when(step == last)
    def _():
        for t in range(TILES):
            prepare, blocks, end = output(t)
            for run in [prepare] + blocks + [end]:
                run()


def local(q, k, v, c, short_taps, residues, rates):
    length, wide = q.shape
    taps = short_taps.shape[1]
    span = taps - 1
    groups, modes = residues.shape
    members = wide // groups
    ctx = lax.axis_size("ctx")
    tiles = wide // LANES
    per = LANES // members
    width = per * modes
    rows = length // BLOCK * members
    lanes = per * BLOCK
    sizes = (members, modes, taps, ctx)
    me = lax.axis_index("ctx").astype(jnp.int32).reshape(1)
    prior = lax.ppermute(
        jnp.concatenate([q[length - span :], k[length - span :], v[length - span :]], axis=0),
        "ctx", [(i, i + 1) for i in range(ctx - 1)],
    )
    after = lax.ppermute(
        jnp.concatenate([q[:span], k[:span], v[:span], c[:span]], axis=0),
        "ctx", [(i + 1, i) for i in range(ctx - 1)],
    )

    smem = pl.BlockSpec(memory_space=pltpu.SMEM)
    stream = pl.BlockSpec((length, TILES * LANES), lambda i: (0, i))
    tap_spec = pl.BlockSpec((3, taps, TILES * LANES), lambda i: (0, 0, i))
    group_spec = pl.BlockSpec((TILES * per, modes), lambda i: (i, 0))
    row = pl.BlockSpec((TILES, 1, width), lambda i: (i, 0, 0))
    turned = pl.BlockSpec((TILES * rows, lanes), lambda i: (i, 0))
    ends = pl.BlockSpec((TILES * rows, width), lambda i: (i, 0))
    swap = pl.BlockSpec((ctx, TILES * members, width), lambda i: (0, i, 0))

    def strip(n):
        return pl.BlockSpec((n, TILES * LANES), lambda i: (0, i))

    turned_shape = jax.ShapeDtypeStruct((tiles * rows, lanes), BF16)
    ends_shape = jax.ShapeDtypeStruct((tiles * rows, width), F32)
    big = jax.ShapeDtypeStruct((length, wide), BF16)
    x, h, ef, eb, send, *kept = pl.pallas_call(
        functools.partial(states_kernel, sizes),
        grid=(tiles // TILES,),
        in_specs=[smem, stream, stream, stream, stream, strip(3 * span), tap_spec, group_spec],
        out_specs=[turned, turned, ends, ends, swap] + [stream] * len(KEPT),
        out_shape=[
            turned_shape, turned_shape, ends_shape, ends_shape,
            jax.ShapeDtypeStruct((ctx, tiles * members, width), F32),
        ] + [big] * len(KEPT),
        scratch_shapes=[
            pltpu.VMEM((TILES, 3, PAD + length, LANES), F32),
            pltpu.VMEM((TILES, length, LANES), BF16),
            pltpu.VMEM((TILES, length, LANES), BF16),
            pltpu.VMEM((TILES, lanes, 2 * width), BF16),
            pltpu.VMEM((TILES, lanes, 2 * width), BF16),
        ],
        cost_estimate=pl.CostEstimate(flops=4 * 10**9, bytes_accessed=34 * 10**6, transcendentals=0),
        name="states",
    )(me, q, k, v, c, prior, short_taps, rates)
    recv = lax.all_to_all(send, "ctx", split_axis=0, concat_axis=0, tiled=True)
    lag = pl.pallas_call(
        functools.partial(pairs_kernel, sizes),
        grid=(tiles // TILES,),
        in_specs=[turned, turned, group_spec],
        out_specs=row,
        out_shape=jax.ShapeDtypeStruct((tiles, 1, width), F32),
        cost_estimate=pl.CostEstimate(flops=4 * 10**9, bytes_accessed=17 * 10**6, transcendentals=0),
        name="pairs",
    )(x, h, rates)
    steps = tiles // TILES

    def late(spec):
        return pl.BlockSpec(spec.block_shape, lambda i: spec.index_map(jnp.maximum(i - 1, 0)))

    def soon(spec):
        return pl.BlockSpec(spec.block_shape, lambda i: spec.index_map(jnp.minimum(i, steps - 1)))

    lines = late(stream)
    mixed, gq, gk, gv, terms = pl.pallas_call(
        functools.partial(finish_kernel, sizes),
        grid=(steps + 1,),
        in_specs=[
            smem, lines, lines, lines, lines, late(strip(3 * span)), late(strip(4 * span)),
            late(tap_spec), soon(group_spec), soon(group_spec), soon(row), soon(turned),
            soon(turned), soon(ends), soon(ends), soon(swap),
        ] + [lines] * len(KEPT),
        out_specs=[
            lines, lines, lines, lines,
            late(pl.BlockSpec((ctx, 16, TILES * LANES), lambda i: (0, 0, i))),
        ],
        out_shape=[big, big, big, big, jax.ShapeDtypeStruct((ctx, 16, wide), BF16)],
        scratch_shapes=[
            pltpu.VMEM((TILES, 3, 2 * PAD + length, LANES), F32),
            pltpu.VMEM((TILES, 3, PAD + length, LANES), F32),
            pltpu.VMEM((TILES, 2, per, BLOCK, BLOCK), BF16),
            pltpu.VMEM((TILES, 2, per, width, BLOCK), BF16),
            pltpu.VMEM((TILES, 2, length // BLOCK, LANES, BLOCK), F32),
            pltpu.VMEM((2, TILES, 3, PAD, LANES), F32),
            pltpu.VMEM((TILES, length, LANES), F32),
            pltpu.VMEM((TILES, length, LANES), F32),
        ],
        cost_estimate=pl.CostEstimate(flops=8 * 10**9, bytes_accessed=50 * 10**6, transcendentals=0),
        name="finish",
    )(me, q, k, v, c, prior, after, short_taps, rates, residues, lag, x, h, ef, eb, recv, *kept)
    total = jnp.sum(
        lax.all_to_all(terms, "ctx", split_axis=0, concat_axis=0, tiled=True).astype(F32), axis=0
    )
    count = 3 * taps
    grad_taps = total[:count].reshape(3, taps, wide)
    grad_res = (total[count] + total[count + 1]).reshape(groups, modes)
    return mixed, gq, gk, gv, grad_taps, grad_res


def solution(mesh):
    stream = P("ctx", "tp")
    return jax.shard_map(
        local,
        mesh=mesh,
        in_specs=(stream, stream, stream, stream, P(None, None, "tp"), P("tp", None), P("tp", None)),
        out_specs=(stream, stream, stream, stream, P(None, None, "tp"), P("tp", None)),
        check_vma=False,
    )
```

```python
import functools
import jax
import jax.numpy as jnp
from jax import lax
from jax.experimental import pallas as pl
from jax.experimental.pallas import tpu as pltpu
from jax.sharding import PartitionSpec as P

F32 = jnp.float32
BF16 = jnp.bfloat16
BLOCK = 128
LANES = 128
TILES = 2
WIDE = 4
PAD = 8
PART = 64
KEPT = (0, 1, 2)


def dot(a, b, a_dim=1, b_dim=0, precision=None):
    return lax.dot_general(
        a, b, (((a_dim,), (b_dim,)), ((), ())), precision=precision, preferred_element_type=F32
    )


def iota(shape, axis):
    return lax.broadcasted_iota(jnp.int32, shape, axis)


def split(value):
    high = value.astype(BF16)
    return high, (value - high.astype(F32)).astype(BF16)


def mask(condition):
    return condition.astype(F32).astype(BF16)


def eye():
    shape = (BLOCK, BLOCK)
    return mask(iota(shape, 0) == iota(shape, 1))


def fine_dot(a, b, a_dim=1, b_dim=0):
    rows = a.shape[0]
    a_high, a_low = split(a)
    b_high, b_low = split(b)
    wide = dot(jnp.concatenate([a_high, a_low], axis=0), b_high, a_dim, b_dim)
    return wide[:rows] + (wide[rows:] + dot(a_high, b_low, a_dim, b_dim))


def as_row(value):
    groups, modes = value.shape
    width = groups * modes
    pick = mask(iota((modes, width), 1) % modes == iota((modes, width), 0))
    high = value.astype(BF16).astype(F32)
    middle = (value - high).astype(BF16).astype(F32)
    low = value - high - middle
    wide = dot(jnp.concatenate([high, middle, low], axis=0).astype(BF16), pick)
    own = iota((3 * groups, width), 1) // modes == iota((3 * groups, width), 0) % groups
    wide = jnp.where(own, wide, 0.0)
    parts = [
        jnp.sum(wide[i * groups : (i + 1) * groups], axis=0, keepdims=True) for i in range(3)
    ]
    return parts[0] + (parts[1] + parts[2])


def powers(rate_row, first, down):
    width = rate_row.shape[1]
    row = iota((8, width), 0).astype(F32)
    lag = 7.0 - row if down else row
    part = jnp.exp(-rate_row * (lag + first))
    factor = jnp.exp(-rate_row * 8.0)
    parts = [part]
    for _ in range(BLOCK // 8 - 1):
        parts.append(parts[-1] * factor)
    return jnp.concatenate(parts[::-1] if down else parts, axis=0)


def fill_streams(streams, prior_ref, us, length):
    span = prior_ref.shape[0] // len(streams)
    for i, ref in enumerate(streams):
        us[i, PAD - span : PAD, :] = prior_ref[i * span : (i + 1) * span, :].astype(F32)
        us[i, PAD : PAD + length, :] = ref[...].astype(F32)


def windows(us, i, start, rows, taps):
    return [us[i, PAD + start - j : PAD + start - j + rows, :] for j in range(taps)]


def short(taps_ref, i, wins):
    total = taps_ref[i, 0:1, :] * wins[0]
    for j in range(1, len(wins)):
        total = total + taps_ref[i, j : j + 1, :] * wins[j]
    return total


def states_tile(
    sizes, me, q_ref, k_ref, v_ref, c_ref, prior_ref, taps_ref, rates,
    x_ref, h_ref, ef_ref, eb_ref, send_ref, short_refs, us, gs, ls, af, ab,
):
    members, modes, taps, ctx = sizes
    length = q_ref.shape[0]
    count, groups = length // BLOCK, LANES // members
    width = groups * modes
    unit = eye()
    rate = as_row(rates)
    fill_streams((q_ref, k_ref, v_ref), prior_ref, us, length)
    half = BLOCK // 2
    for n in range(count):
        for part in range(2):
            start = n * BLOCK + part * half
            rows = slice(start, start + half)
            shorts = [short(taps_ref, i, windows(us, i, start, half, taps)) for i in range(3)]
            shorts = [value.astype(BF16) for value in shorts]
            for i, ref in short_refs.items():
                ref[rows, :] = shorts[i]
            gs[rows, :] = shorts[1] * shorts[2]
            ls[rows, :] = c_ref[rows, :] * shorts[0]
        if n % 2 == 0 and n + 1 < count:
            continue
        blocks = [n - 1, n] if n % 2 else [n]
        for source, target in ((gs, x_ref), (ls, h_ref)):
            rows = slice(blocks[0] * BLOCK, (n + 1) * BLOCK)
            turned = dot(unit, source[rows, :], 1, 1).astype(BF16)
            for at, m in enumerate(blocks):
                for g in range(groups):
                    target[m * members : (m + 1) * members, g * BLOCK : (g + 1) * BLOCK] = turned[
                        g * members : (g + 1) * members, at * BLOCK : (at + 1) * BLOCK
                    ]
        if n == 1:
            for table, array in ((af, powers(rate, 0.0, True)), (ab, powers(rate, 0.0, False))):
                both = jnp.concatenate(split(array), axis=1)
                lane_group = iota(both.shape, 1) % width // modes
                for g in range(groups):
                    table[g * BLOCK : (g + 1) * BLOCK, :] = both * mask(lane_group == g)
    decay = jnp.exp(-rate * float(BLOCK))
    forward = dot(x_ref[...], af[...])
    forward = forward[:, :width] + forward[:, width:]
    backward = dot(h_ref[...], ab[...])
    backward = backward[:, :width] + backward[:, width:]
    ef_ref[...] = forward
    eb_ref[...] = backward
    last = jnp.zeros((members, width), F32)
    first = jnp.zeros((members, width), F32)
    for n in range(count):
        m = count - 1 - n
        last = decay * last + forward[n * members : (n + 1) * members]
        first = decay * first + backward[m * members : (m + 1) * members]
    for j in range(ctx):
        send_ref[j] = jnp.where(j > me, last, first)


def states_kernel(sizes, *refs):
    members, modes, taps, ctx = sizes
    me_ref, q_ref, k_ref, v_ref, c_ref, prior_ref, taps_ref, rate_ref = refs[:8]
    x_ref, h_ref, ef_ref, eb_ref, send_ref = refs[8:13]
    kept = refs[13 : 13 + len(KEPT)]
    us, gs, ls, af, ab = refs[13 + len(KEPT) :]
    groups = LANES // members
    rows = x_ref.shape[0] // WIDE
    for t in range(WIDE):
        lanes, part = pl.ds(t * LANES, LANES), pl.ds(t * rows, rows)
        states_tile(
            sizes, me_ref[0],
            *[r.at[:, lanes] for r in (q_ref, k_ref, v_ref, c_ref, prior_ref)],
            taps_ref.at[:, :, lanes], rate_ref[t * groups : (t + 1) * groups, :],
            *[r.at[part, :] for r in (x_ref, h_ref, ef_ref, eb_ref)],
            send_ref.at[:, pl.ds(t * members, members), :],
            {i: r.at[:, lanes] for i, r in zip(KEPT, kept)},
            us.at[t], gs.at[t], ls.at[t], af.at[t], ab.at[t],
        )


def pairs_tile(sizes, x_ref, h_ref, rates, grad_ref):
    members, modes, taps, ctx = sizes
    groups = LANES // members
    width = groups * modes
    rate = as_row(rates)
    row, col = iota((BLOCK, BLOCK), 0), iota((BLOCK, BLOCK), 1)
    causal = row + col < BLOCK
    flip = mask(row + col == BLOCK - 1)
    sums = []
    for p in range(0, groups, 2):
        pair = range(p, min(p + 2, groups))
        stack = [h_ref[:, g * BLOCK : (g + 1) * BLOCK] for g in pair]
        turned = dot(flip, jnp.concatenate(stack, axis=0), 1, 1).astype(BF16)
        for at, g in enumerate(pair):
            x = x_ref[:, g * BLOCK : (g + 1) * BLOCK]
            rows = x.shape[0]
            pairs = jnp.where(causal, dot(turned[:, at * rows : (at + 1) * rows], x), 0.0)
            total = pairs[0:8]
            for i in range(1, BLOCK // 8):
                total = total + pltpu.roll(pairs[8 * i : 8 * i + 8], 8 * i, 1)
            sums.append(pltpu.roll(total, 0, 1, stride=1, stride_axis=0))
    crossed = fine_dot(jnp.concatenate(sums, axis=0), powers(rate, 0.0, True))
    shape = (8 * groups, width)
    grad_ref[...] = jnp.sum(
        jnp.where(iota(shape, 1) // modes == iota(shape, 0) // 8, crossed, 0.0), axis=0, keepdims=True
    )


def pairs_kernel(sizes, x_ref, h_ref, rate_ref, grad_ref):
    groups = LANES // sizes[0]
    rows = x_ref.shape[0] // TILES
    for t in range(TILES):
        part, own = pl.ds(t * rows, rows), slice(t * groups, (t + 1) * groups)
        pairs_tile(sizes, x_ref.at[part, :], h_ref.at[part, :], rate_ref[own, :], grad_ref.at[t])


def conv_steps(
    sizes, length, me, rates, residues, lag_ref, x_ref, h_ref, ef_ref, eb_ref, recv_ref,
    ts, rs, turn, note,
):
    members, modes, taps, ctx = sizes
    count, groups = length // BLOCK, LANES // members
    width = groups * modes
    rate, res = as_row(rates), as_row(residues)
    states, lefts, own = [], {}, {}

    def prepare():
        whole, decay = jnp.exp(-rate * float(length)), jnp.exp(-rate * float(BLOCK))
        ahead = jnp.zeros((members, width), F32)
        behind = jnp.zeros((members, width), F32)
        for i in range(ctx - 1):
            j = ctx - 1 - i
            ahead = jnp.where(i < me, whole * ahead + recv_ref[i], ahead)
            behind = jnp.where(j > me, whole * behind + recv_ref[j], behind)
        incoming = behind
        forward, backward = [], [None] * count
        for n in range(count):
            m = count - 1 - n
            forward.append(ahead)
            ahead = decay * ahead + ef_ref[n * members : (n + 1) * members, :]
            backward[m] = behind
            behind = decay * behind + eb_ref[m * members : (m + 1) * members, :]
        cross = forward[0] * eb_ref[0:members, :]
        for n in range(1, count):
            cross = cross + forward[n] * eb_ref[n * members : (n + 1) * members, :]
        states.extend((forward, backward))

        order = iota((PAD, width), 0).astype(F32)
        lane_group = iota((members, width), 1) // modes
        channel_own = iota((groups, LANES), 1) // members == iota((groups, LANES), 0)

        def spread(state):
            return jnp.concatenate(
                [jnp.where(lane_group == g, state, 0.0) for g in range(groups)], axis=0
            )

        def near(shift):
            sums = jnp.sum(residues * jnp.exp(-rates * shift), axis=1, keepdims=True)
            return jnp.sum(jnp.where(channel_own, sums, 0.0), axis=0, keepdims=True)

        note[0] = fine_dot(res * jnp.exp(-rate * (order + 1.0)), spread(ahead), 1, 1)
        note[1] = fine_dot(res * jnp.exp(rate * order), spread(incoming), 1, 1)
        note[2, 0:1, :] = near(0.0)
        note[2, 1:2, :] = near(1.0)
        note[2, 2:3, :] = near(-1.0)
        note[2, 3:4, :] = (
            jnp.exp(-rate) * jnp.sum(cross, axis=0, keepdims=True) + lag_ref[...]
        )

    def begin(d):
        down = d == 1
        mine = iota((groups, width), 1) // modes == iota((groups, width), 0)
        response = fine_dot(jnp.where(mine, res, 0.0), powers(rate, 0.0, down), 1, 1)
        high, low = split(jnp.transpose(res * powers(rate, 1.0, down)))
        state = jnp.concatenate(states[d], axis=0)
        wide = state.astype(BF16).astype(F32)
        fine = pltpu.roll(state - wide, 2 * modes, 1)
        again = pltpu.roll(wide, 4 * modes, 1)
        own[d] = (response, high, low, wide, fine, again)

    def group(d, g):
        down = d == 1
        response, high, low, wide, fine, again = own[d]
        square = (BLOCK, BLOCK)
        keep = iota(square, 1) <= iota(square, 0) if down else iota(square, 1) >= iota(square, 0)
        line = jnp.broadcast_to(response[g : g + 1], (8, BLOCK))
        line = pltpu.roll(line, int(down), 1, stride=1, stride_axis=0)
        parts = [line] + [pltpu.roll(line, 8 * i, 1) for i in range(1, BLOCK // 8)]
        ts[d, g] = jnp.concatenate(parts, axis=0).astype(BF16) * mask(keep)
        rows = slice(g * modes, (g + 1) * modes)
        for turns, piece in ((0, high), (1, high), (2, low)):
            at = (g * modes + 2 * modes * turns) % width
            rs[d, g, at : at + modes, :] = piece[rows]
        if g % 2 == 0:
            p = g // 2
            quarter = iota((count * members, width), 1) // (2 * modes)
            lefts[d] = jnp.where(
                quarter == p, wide, jnp.where(quarter == (p + 1) % 4, fine, again)
            ).astype(BF16)
        source = (x_ref, h_ref)[d]
        both = jnp.concatenate([source[:, g * BLOCK : (g + 1) * BLOCK], lefts[d]], axis=1)
        out = dot(both, jnp.concatenate([ts[d, g], rs[d, g]], axis=0))
        for n in range(count):
            turn[d, n, g * members : (g + 1) * members, :] = out[n * members : (n + 1) * members]

    steps = [prepare]
    for d in range(2):
        steps.append(functools.partial(begin, d))
        steps.extend(functools.partial(group, d, g) for g in range(groups))
    return steps


def turn_steps(length, turn, lo, gg):
    def step(n):
        rows = slice(n * BLOCK, (n + 1) * BLOCK)
        lo[rows, :] = jnp.transpose(turn[0, n])
        gg[rows, :] = jnp.transpose(turn[1, n])

    return [functools.partial(step, n) for n in reversed(range(length // BLOCK))]


def output_steps(
    sizes, q_ref, k_ref, v_ref, c_ref, prior_ref, after_ref, taps_ref, short_refs,
    mixed_ref, gq_ref, gk_ref, gv_ref, terms_ref, us, es, note, lo, gg,
):
    members, modes, taps, ctx = sizes
    length = q_ref.shape[0]
    count = length // BLOCK
    span = taps - 1
    streams = (q_ref, k_ref, v_ref)
    part = PART
    ones = jnp.ones((8, BLOCK), BF16)
    sums = [jnp.zeros((8, LANES), F32) for _ in range(3 * taps)]

    def prepare():
        head = after_ref[...].astype(F32)
        rest = jnp.zeros((PAD - span, LANES), F32)
        ends = []
        for i in range(3):
            if i in short_refs:
                us[i, PAD + length - span : PAD + length, :] = streams[i][
                    length - span :, :
                ].astype(F32)
            else:
                us[i, PAD - span : PAD, :] = prior_ref[i * span : (i + 1) * span, :].astype(F32)
                us[i, PAD : PAD + length, :] = streams[i][...].astype(F32)
            us[i, PAD + length : 2 * PAD + length, :] = jnp.concatenate(
                [head[i * span : (i + 1) * span], rest], axis=0
            )
            ends.append(short(taps_ref, i, windows(us, i, length, PAD, taps)))
        query, key, value = ends
        cot = jnp.concatenate([head[3 * span : 4 * span], rest], axis=0)
        line = jnp.zeros((1, LANES), F32)
        second = iota((PAD, LANES), 0) == 1
        gated = (key * value).astype(BF16).astype(F32)
        grad_long = (cot * query).astype(BF16).astype(F32)
        gated_prev = jnp.where(second, jnp.concatenate([line, gated[:-1]], axis=0), 0.0)
        grad_prev = jnp.where(second, jnp.concatenate([line, grad_long[:-1]], axis=0), 0.0)
        out = note[0] + note[2, 0:1, :] * gated + note[2, 1:2, :] * gated_prev
        back = note[1] - note[2, 2:3, :] * grad_prev
        for i, edge in enumerate((cot * out, back * value, back * key)):
            es[i, length : length + PAD, :] = edge

    def tap(i, j):
        return jnp.broadcast_to(taps_ref[i, j : j + 1, :], (16, LANES)).astype(BF16)

    def scale(value, row):
        return (value.reshape(value.shape[0] // 16, 16, LANES) * row[None]).reshape(value.shape)

    tap_rows = [[tap(i, j) for j in range(taps)] for i in range(3)]

    def block(n):
        products = [[] for _ in range(3 * taps)]
        for start in reversed(range(n * BLOCK, (n + 1) * BLOCK, part)):
            rows = slice(start, start + part)
            long_out, grad_gated = lo[rows, :], gg[rows, :]
            key, value = [short_refs[i][rows, :].astype(F32) for i in (1, 2)]
            mixed_ref[rows, :] = short_refs[0][rows, :] * long_out.astype(BF16)
            edges = (c_ref[rows, :].astype(F32) * long_out, grad_gated * value, grad_gated * key)
            for i, (edge, target) in enumerate(zip(edges, (gq_ref, gk_ref, gv_ref))):
                es[i, rows, :] = edge
                stream = streams[i][rows, :]
                total = None
                for j in range(taps):
                    later = (es[i, start + j : start + j + part, :] if j else edge).astype(BF16)
                    products[i * taps + j].insert(0, later * stream)
                    term = scale(later, tap_rows[i][j])
                    total = term if total is None else total + term
                target[rows, :] = total
        for a in range(0, 3 * taps, 2):
            wide = [jnp.concatenate(p, axis=0) for p in products[a : a + 2]]
            added = dot(ones, jnp.concatenate(wide, axis=1))
            for at in range(len(wide)):
                sums[a + at] = sums[a + at] + added[:, at * LANES : (at + 1) * LANES]

    def end():
        high, low = split(note[2, 3:4, :])
        lines = [s[0:1] for s in sums] + [high.astype(F32), low.astype(F32)]
        lines.append(jnp.zeros((16 - len(lines), LANES), F32))
        terms = jnp.concatenate(lines, axis=0).astype(BF16)
        for j in range(ctx):
            terms_ref[j] = terms

    blocks = [functools.partial(block, n) for n in reversed(range(count))]
    return prepare, blocks, end


def finish_kernel(sizes, *refs):
    members = sizes[0]
    me_ref, q_ref, k_ref, v_ref, c_ref, prior_ref, after_ref, taps_ref, rate_ref, res_ref = refs[:10]
    lag_ref, x_ref, h_ref, ef_ref, eb_ref, recv_ref = refs[10:16]
    kept, rest = refs[16 : 16 + len(KEPT)], refs[16 + len(KEPT) :]
    mixed_ref, gq_ref, gk_ref, gv_ref, terms_ref, us, es, ts, rs, turn, note, lo, gg = rest
    length = q_ref.shape[0]
    groups = LANES // members
    rows = x_ref.shape[0] // TILES
    step, last = pl.program_id(0), pl.num_programs(0) - 1

    def convolve(t):
        part, own = pl.ds(t * rows, rows), slice(t * groups, (t + 1) * groups)
        return conv_steps(
            sizes, length, me_ref[0], rate_ref[own, :], res_ref[own, :], lag_ref.at[t],
            *[r.at[part, :] for r in (x_ref, h_ref, ef_ref, eb_ref)],
            recv_ref.at[:, pl.ds(t * members, members), :],
            ts.at[t], rs.at[t], turn.at[t], note.at[1, t],
        )

    def output(t):
        lanes = pl.ds(t * LANES, LANES)
        return output_steps(
            sizes, *[r.at[:, lanes] for r in (q_ref, k_ref, v_ref, c_ref, prior_ref, after_ref)],
            taps_ref.at[:, :, lanes], {i: r.at[:, lanes] for i, r in zip(KEPT, kept)},
            *[r.at[:, lanes] for r in (mixed_ref, gq_ref, gk_ref, gv_ref)],
            terms_ref.at[:, :, lanes], us.at[t], es.at[t], note.at[0, t], lo.at[t], gg.at[t],
        )

    def settle(t):
        note[0, t] = note[1, t]

    @pl.when(step == 0)
    def _():
        rs[...] = jnp.zeros_like(rs)
        for t in range(TILES):
            for run in convolve(t) + turn_steps(length, turn.at[t], lo.at[t], gg.at[t]):
                run()
            settle(t)

    @pl.when((step > 0) & (step < last))
    def _():
        for t in range(TILES):
            prepare, blocks, end = output(t)
            work = convolve(t)
            turns = turn_steps(length, turn.at[t], lo.at[t], gg.at[t])
            early = len(blocks)
            share = -(-len(work) // early)
            prepare()
            ready = 0
            for k, block in enumerate(blocks):
                for run in work[k * share : (k + 1) * share]:
                    run()
                block()
                if (k + 1) * share >= len(work):
                    while ready <= k and ready < (k + 1 - early) * 2 + 2:
                        turns[ready]()
                        ready += 1
            for run in turns[ready:]:
                run()
            end()
            settle(t)

    @pl.when(step == last)
    def _():
        for t in range(TILES):
            prepare, blocks, end = output(t)
            for run in [prepare] + blocks + [end]:
                run()


def local(q, k, v, c, short_taps, residues, rates):
    length, wide = q.shape
    taps = short_taps.shape[1]
    span = taps - 1
    groups, modes = residues.shape
    members = wide // groups
    ctx = lax.axis_size("ctx")
    tiles = wide // LANES
    per = LANES // members
    width = per * modes
    rows = length // BLOCK * members
    lanes = per * BLOCK
    sizes = (members, modes, taps, ctx)
    me = lax.axis_index("ctx").astype(jnp.int32).reshape(1)
    prior = lax.ppermute(
        jnp.concatenate([q[length - span :], k[length - span :], v[length - span :]], axis=0),
        "ctx", [(i, i + 1) for i in range(ctx - 1)],
    )
    after = lax.ppermute(
        jnp.concatenate([q[:span], k[:span], v[:span], c[:span]], axis=0),
        "ctx", [(i + 1, i) for i in range(ctx - 1)],
    )

    smem = pl.BlockSpec(memory_space=pltpu.SMEM)
    stream = pl.BlockSpec((length, TILES * LANES), lambda i: (0, i))
    tap_spec = pl.BlockSpec((3, taps, TILES * LANES), lambda i: (0, 0, i))
    group_spec = pl.BlockSpec((TILES * per, modes), lambda i: (i, 0))
    row = pl.BlockSpec((TILES, 1, width), lambda i: (i, 0, 0))
    turned = pl.BlockSpec((TILES * rows, lanes), lambda i: (i, 0))
    ends = pl.BlockSpec((TILES * rows, width), lambda i: (i, 0))
    swap = pl.BlockSpec((ctx, TILES * members, width), lambda i: (0, i, 0))

    def strip(n):
        return pl.BlockSpec((n, TILES * LANES), lambda i: (0, i))

    turned_shape = jax.ShapeDtypeStruct((tiles * rows, lanes), BF16)
    ends_shape = jax.ShapeDtypeStruct((tiles * rows, width), F32)
    big = jax.ShapeDtypeStruct((length, wide), BF16)
    def widen(spec):
        shape, moved = list(spec.block_shape), spec.index_map(1)
        at = [j for j, step in enumerate(moved) if not isinstance(step, int) or step == 1][0]
        shape[at] = shape[at] // TILES * WIDE
        return pl.BlockSpec(tuple(shape), spec.index_map)

    x, h, ef, eb, send, *kept = pl.pallas_call(
        functools.partial(states_kernel, sizes),
        grid=(tiles // WIDE,),
        in_specs=[smem] + [widen(p) for p in (stream,) * 4 + (strip(3 * span), tap_spec, group_spec)],
        out_specs=[widen(p) for p in (turned, turned, ends, ends, swap) + (stream,) * len(KEPT)],
        out_shape=[
            turned_shape, turned_shape, ends_shape, ends_shape,
            jax.ShapeDtypeStruct((ctx, tiles * members, width), F32),
        ] + [big] * len(KEPT),
        scratch_shapes=[
            pltpu.VMEM((WIDE, 3, PAD + length, LANES), F32),
            pltpu.VMEM((WIDE, length, LANES), BF16),
            pltpu.VMEM((WIDE, length, LANES), BF16),
            pltpu.VMEM((WIDE, lanes, 2 * width), BF16),
            pltpu.VMEM((WIDE, lanes, 2 * width), BF16),
        ],
        cost_estimate=pl.CostEstimate(flops=4 * 10**9, bytes_accessed=34 * 10**6, transcendentals=0),
        name="states",
    )(me, q, k, v, c, prior, short_taps, rates)
    recv = lax.all_to_all(send, "ctx", split_axis=0, concat_axis=0, tiled=True)
    lag = pl.pallas_call(
        functools.partial(pairs_kernel, sizes),
        grid=(tiles // TILES,),
        in_specs=[turned, turned, group_spec],
        out_specs=row,
        out_shape=jax.ShapeDtypeStruct((tiles, 1, width), F32),
        cost_estimate=pl.CostEstimate(flops=4 * 10**9, bytes_accessed=17 * 10**6, transcendentals=0),
        name="pairs",
    )(x, h, rates)
    steps = tiles // TILES

    def late(spec):
        return pl.BlockSpec(spec.block_shape, lambda i: spec.index_map(jnp.maximum(i - 1, 0)))

    def soon(spec):
        return pl.BlockSpec(spec.block_shape, lambda i: spec.index_map(jnp.minimum(i, steps - 1)))

    lines = late(stream)
    mixed, gq, gk, gv, terms = pl.pallas_call(
        functools.partial(finish_kernel, sizes),
        grid=(steps + 1,),
        in_specs=[
            smem, lines, lines, lines, lines, late(strip(3 * span)), late(strip(4 * span)),
            late(tap_spec), soon(group_spec), soon(group_spec), soon(row), soon(turned),
            soon(turned), soon(ends), soon(ends), soon(swap),
        ] + [lines] * len(KEPT),
        out_specs=[
            lines, lines, lines, lines,
            late(pl.BlockSpec((ctx, 16, TILES * LANES), lambda i: (0, 0, i))),
        ],
        out_shape=[big, big, big, big, jax.ShapeDtypeStruct((ctx, 16, wide), BF16)],
        scratch_shapes=[
            pltpu.VMEM((TILES, 3, 2 * PAD + length, LANES), F32),
            pltpu.VMEM((TILES, 3, PAD + length, LANES), F32),
            pltpu.VMEM((TILES, 2, per, BLOCK, BLOCK), BF16),
            pltpu.VMEM((TILES, 2, per, width, BLOCK), BF16),
            pltpu.VMEM((TILES, 2, length // BLOCK, LANES, BLOCK), F32),
            pltpu.VMEM((2, TILES, 3, PAD, LANES), F32),
            pltpu.VMEM((TILES, length, LANES), F32),
            pltpu.VMEM((TILES, length, LANES), F32),
        ],
        cost_estimate=pl.CostEstimate(flops=8 * 10**9, bytes_accessed=50 * 10**6, transcendentals=0),
        name="finish",
    )(me, q, k, v, c, prior, after, short_taps, rates, residues, lag, x, h, ef, eb, recv, *kept)
    total = jnp.sum(
        lax.all_to_all(terms, "ctx", split_axis=0, concat_axis=0, tiled=True).astype(F32), axis=0
    )
    count = 3 * taps
    grad_taps = total[:count].reshape(3, taps, wide)
    grad_res = (total[count] + total[count + 1]).reshape(groups, modes)
    return mixed, gq, gk, gv, grad_taps, grad_res


def solution(mesh):
    stream = P("ctx", "tp")
    return jax.shard_map(
        local,
        mesh=mesh,
        in_specs=(stream, stream, stream, stream, P(None, None, "tp"), P("tp", None), P("tp", None)),
        out_specs=(stream, stream, stream, stream, P(None, None, "tp"), P("tp", None)),
        check_vma=False,
    )
```
